512 devices in a mesh: ctx: 32 (over x, y), pair: 16 (over z, core).
Axes of the slice: x: 4, y: 8, z: 8, core: 2. Of those that a mesh axis runs over, the one named last changes fastest.
Arguments:
- prompt_x: bfloat16 [2, 8192, 16384], P(None, 'ctx', 'pair'), may hold values from -6 to 6
- prompt_bc: bfloat16 [2, 2, 16, 8192], P(None, None, None, 'ctx'), may hold values from -3 to 3
- prompt_logdec: float32 [2, 256, 8192], P(None, 'pair', 'ctx'), may hold values from -2.5 to 0, as said below
- branch_x: bfloat16 [32, 512, 16384], P('pair', None, 'ctx'), may hold values from -6 to 6
- branch_bc: bfloat16 [2, 32, 16, 512], P(None, 'pair'), may hold values from -3 to 3
- branch_logdec: float32 [32, 256, 512], P('pair', 'ctx'), may hold values from -2.5 to 0, as said below
- branch_prompt: int32 [16], P('pair'), may hold values from 0 to 1
- branch_len: int32 [32], P('pair'), may hold values from 128 to 512, as said below
Outputs:
- prompt_y: bfloat16 [2, 8192, 16384], P(None, 'ctx', 'pair')
- branch_y: bfloat16 [32, 512, 16384], P('pair', None, 'ctx')
The draws below stay inside these ranges and needn't reach their ends.
Inputs may be any that keep to these rules, and one draw needn't show every extreme that they name: `prompt_logdec`: the logarithm of a position's decay for each head. `branch_logdec`: the logarithm of a position's decay for each head. `branch_len`: positions of a branch at or after its length are masked; some branch has all 512 positions live.
All inputs are finite; a program needn't handle non-finite values.
Results may differ from the reference program's by a relative error of at most 0.0049.
Values sent between devices are 32-bit elements; how exact they have to be, the bound alone decides.
A program may use at most 64 MiB of HBM per device.

```python
import math
import jax
import jax.numpy as jnp
from jax import lax

H = 256
P_SIZE = 64
N = 16
W = 16384
NPROMPT = 2
TP_DEV = 256
LB = 512
LP = 8192
NPAIR = 16
BR = 32
BLOCK = 256


def head_rates(key):
    key_kind, key_slow, key_fast = jax.random.split(jax.random.fold_in(key, 4242), 3)
    chain_len = LP + LB
    slow_share = 0.5
    coin = jax.random.uniform(key_kind, (H,))
    slow_rate = jnp.exp(jax.random.uniform(key_slow, (H,), minval=math.log(0.05 / chain_len), maxval=math.log(0.8 / chain_len)))
    fast_rate = jnp.exp(jax.random.uniform(key_fast, (H,), minval=math.log(1.0 / 400.0), maxval=math.log(1.0 / 8.0)))
    return jnp.where(coin < slow_share, slow_rate, fast_rate)


def decay_rule(key, label_marker, count_of_rows, sequence_length, section_piece, spike_amounts):
    head_decay_speed = head_rates(key)
    key_jit, key_seg, key_position_draw, key_split_point = jax.random.split(jax.random.fold_in(key, label_marker), 4)
    small_noise = jnp.exp(jax.random.uniform(key_jit, (count_of_rows, H, sequence_length), minval=math.log(0.5), maxval=math.log(2.0)))
    multiplier = jnp.exp(jax.random.uniform(key_seg, (count_of_rows, H, sequence_length // section_piece), minval=math.log(0.5), maxval=math.log(2.0)))
    multiplier = jnp.repeat(multiplier, section_piece, axis=2, total_repeat_length=sequence_length)
    token_positions = jax.random.randint(key_position_draw, (count_of_rows, spike_amounts), 0, sequence_length)
    split_points = jnp.log(jax.random.uniform(key_split_point, (count_of_rows, spike_amounts), minval=0.5, maxval=0.8))
    spots_list = jnp.arange(sequence_length, dtype=jnp.int32)
    spike_amount = jnp.sum(jnp.where(spots_list[None, None, :] == token_positions[:, :, None], split_points[:, :, None], 0.0), axis=1)
    return -(head_decay_speed[None, :, None] * small_noise * multiplier) + spike_amount[:, None, :]


def draw_prompt_logdec(key, part):
    return decay_rule(key, 17, NPROMPT, LP, TP_DEV, 2).astype(jnp.float32)


def draw_branch_logdec(key, part):
    return decay_rule(key, 23, BR, LB, LB, 1).astype(jnp.float32)


def draw_branch_len(key, part):
    key_len, key_perm = jax.random.split(jax.random.fold_in(key, 31), 2)
    values = jax.random.randint(key_len, (BR,), LB // 4, LB + 1)
    order = jax.random.permutation(key_perm, BR)
    values = values.at[order[0]].set(LB)
    values = values.at[order[1]].set(LB // 4)
    return values.astype(jnp.int32)


def touch_ends(array, own_key, least, largest):
    extent = array.shape
    place = [jax.random.randint(jax.random.fold_in(own_key, axis), (), 0, extent[axis]) for axis in range(len(extent))]
    array = array.at[tuple(place)].set(least)
    longest = extent.index(max(extent))
    place[longest] = (place[longest] + 1) % extent[longest]
    return array.at[tuple(place)].set(largest)


def level_of(stream_key, extent, cuts, smallest, largest):
    gain = 1.0
    for dim, blocks in cuts:
        draws = jax.random.uniform(jax.random.fold_in(jax.random.fold_in(stream_key, 6), dim), (blocks,), jnp.float32, smallest / len(cuts), largest / len(cuts))
        gain = gain * jnp.repeat(jnp.exp(draws), extent[dim] // blocks).reshape((-1,) + (1,) * (len(extent) - 1 - dim))
    return gain


def noise(key, shape, width, limit, cuts=(), kind=jnp.bfloat16):
    level = level_of(key, shape, cuts, -0.22, 0.18) if cuts else 1.0
    values = jax.random.normal(key, shape, jnp.float32) * width * level
    return jnp.minimum(jnp.maximum(values, -limit), limit).astype(kind)


def setup_inputs(seed: int = 0) -> dict:
    keys = jax.random.split(jax.random.key(seed), 9)
    return {
        "prompt_x": noise(keys[0], (NPROMPT, LP, W), 1.0, 6.0, ((1, 32), (2, 16))),
        "prompt_bc": noise(keys[1], (2, NPROMPT, N, LP), 0.5, 3.0, ((3, 32),)),
        "prompt_logdec": draw_prompt_logdec(jax.random.fold_in(keys[8], 71), 0),
        "branch_x": noise(keys[3], (BR, LB, W), 1.0, 6.0, ((0, 16), (2, 32))),
        "branch_bc": noise(keys[4], (2, BR, N, LB), 0.5, 3.0, ((1, 16),)),
        "branch_logdec": draw_branch_logdec(jax.random.fold_in(keys[8], 71), 0),
        "branch_prompt": touch_ends(jax.random.randint(keys[6], (NPAIR,), 0, NPROMPT), jax.random.fold_in(keys[6], 1), 0, NPROMPT - 1).astype(jnp.int32),
        "branch_len": draw_branch_len(jax.random.fold_in(keys[8], 71), 0),
    }


def block_pass(inputs, log_decay, b_rows, c_rows, start_state):
    block_rows, channels = inputs.shape
    head_count = log_decay.shape[0]
    head_width = channels // head_count
    running = jnp.cumsum(log_decay, axis=1)
    in_gain = jnp.sqrt(-jnp.expm1(2.0 * log_decay))
    scores = jnp.dot(c_rows.T, b_rows, preferred_element_type=jnp.float32)
    row_ids = lax.broadcasted_iota(jnp.int32, (block_rows, block_rows), 0)
    col_ids = lax.broadcasted_iota(jnp.int32, (block_rows, block_rows), 1)
    causal = col_ids <= row_ids
    to_end = jnp.exp(running[:, -1:] - running) * in_gain
    inject = (b_rows.astype(jnp.float32)[None, :, :] * to_end[:, None, :]).astype(jnp.bfloat16)

    def head_pass(head_id):
        running_h = running[head_id]
        columns = lax.dynamic_slice_in_dim(inputs, head_id * head_width, head_width, 1)
        differ = jnp.where(causal, running_h[:, None] - running_h[None, :], 0.0)
        weights = jnp.where(causal, jnp.exp(differ), 0.0)
        weights = (scores * weights * in_gain[head_id][None, :]).astype(jnp.bfloat16)
        inner_out = jnp.dot(weights, columns, preferred_element_type=jnp.float32)
        states = jnp.dot(inject[head_id], columns, preferred_element_type=jnp.float32)
        return (inner_out, states)
    inner_out, states = lax.map(head_pass, jnp.arange(head_count, dtype=jnp.int32))
    inner_out = jnp.transpose(inner_out, (1, 0, 2)).reshape(block_rows, channels)
    projected = jnp.einsum('nt,hnp->thp', c_rows.astype(jnp.float32), start_state, precision=lax.Precision.HIGHEST)
    carried = (projected * jnp.exp(running).T[:, :, None]).reshape(block_rows, channels)
    end_state = jnp.exp(running[:, -1])[:, None, None] * start_state + states
    return (inner_out + carried, end_state)

def run_blocks(inputs, log_decay, b_and_c, start_state):
    sequence_length, channels = inputs.shape
    head_count = log_decay.shape[0]
    state_size = b_and_c.shape[1]
    block_count = sequence_length // BLOCK
    input_blocks = inputs.reshape(block_count, BLOCK, channels)
    decay_blocks = jnp.transpose(log_decay.reshape(head_count, block_count, BLOCK), (1, 0, 2))
    proj_blocks = jnp.transpose(b_and_c.reshape(2, state_size, block_count, BLOCK), (2, 0, 1, 3))

    def advance(carry_state, pieces):
        block_in, block_decay, block_proj = pieces
        block_out, end_state = block_pass(block_in, block_decay, block_proj[0], block_proj[1], carry_state)
        return (end_state, block_out.astype(jnp.bfloat16))
    end_state, outputs = lax.scan(advance, start_state, (input_blocks, decay_blocks, proj_blocks))
    return (outputs.reshape(sequence_length, channels), end_state)

def reference(prompt_x, prompt_bc, prompt_logdec, branch_x, branch_bc, branch_logdec, branch_prompt, branch_len):
    zero_state = jnp.zeros((H, N, P_SIZE), jnp.float32)
    prompt_out = []
    finals = []
    for prompt_id in range(NPROMPT):
        result, end_state = run_blocks(prompt_x[prompt_id], prompt_logdec[prompt_id], prompt_bc[:, prompt_id], zero_state)
        prompt_out.append(result)
        finals.append(end_state)
    finals = jnp.stack(finals)

    def branch_pass(branch_id):
        source = branch_prompt[branch_id // 2]
        start_state = jnp.take(finals, source, axis=0)
        result, end_state = run_blocks(branch_x[branch_id], branch_logdec[branch_id], branch_bc[:, branch_id], start_state)
        live_rows = jnp.arange(LB, dtype=jnp.int32) < branch_len[branch_id]
        return jnp.where(live_rows[:, None], result, jnp.zeros_like(result))
    branch_out = lax.map(branch_pass, jnp.arange(BR, dtype=jnp.int32))
    return (jnp.stack(prompt_out), branch_out)
```

```python
import functools

import jax
import jax.numpy as jnp
from jax import lax
from jax.experimental import pallas as pl
from jax.experimental.pallas import tpu as pltpu
from jax.sharding import Mesh
from jax.sharding import PartitionSpec as P

MESH = pl.DeviceIdType.MESH
CTX = ("ctx_0", "ctx_1")
F32 = jnp.float32
BF16 = jnp.bfloat16
BLOCK = 256
LOG2E = 1.4426950408889634


def iota(shape, dim):
    return lax.broadcasted_iota(jnp.int32, shape, dim)


def dot(a, b):
    return jnp.dot(a, b, preferred_element_type=F32)


def far_first(n):
    return sorted(range(1, n), key=lambda k: -min(k, n - k))


def three_parts(a):
    hi = a.astype(BF16)
    rest = a - hi.astype(F32)
    mid = rest.astype(BF16)
    low = (rest - mid.astype(F32)).astype(BF16)
    return hi, mid, low


def running_sums(rows):
    until = (iota((BLOCK, BLOCK), 0) <= iota((BLOCK, BLOCK), 1)).astype(F32).astype(BF16)
    count = rows.shape[0]
    sums = dot(jnp.concatenate(three_parts(rows), axis=0), until)
    total = sums[:count] + (sums[count : 2 * count] + sums[2 * count :])
    return total * LOG2E


def log_gain(rows):
    z = 2.0 * rows
    series = 1.0 / 362880.0
    for factor in (40320.0, 5040.0, 720.0, 120.0, 24.0, 6.0, 2.0, 1.0):
        series = series * z + 1.0 / factor
    squared = jnp.where(z > -0.5, -z * series, 1.0 - jnp.exp(z))
    return jnp.where(squared > 0.0, (0.5 * LOG2E) * jnp.log(squared), -1e30)


def pair_of(even, odd, low_lanes):
    return jnp.where(low_lanes, even, odd)


def rows16(tile):
    return jnp.concatenate(
        [jnp.broadcast_to(tile[0:1], (16, 128)), jnp.broadcast_to(tile[1:2], (16, 128))], axis=0
    )


def pair_states(b_rows, weights, x_ref, unit_of, heads):
    low16 = iota((16, 128), 1) < 64
    found = []
    for group in range(heads // 4):
        push = jnp.concatenate(
            [b_rows * weights[4 * group + i : 4 * group + i + 1, :] for i in range(4)], axis=0
        ).astype(BF16)
        unit, lane = unit_of(group)
        sums = dot(push, x_ref[unit, :, lane : lane + 256])
        for i in range(2):
            part = sums[32 * i : 32 * i + 32, 128 * i : 128 * i + 128]
            found.append(pair_of(part[0:16], part[16:32], low16))
    return found


def store_parts(ref, index, lane, state):
    for place, part in enumerate(three_parts(state)):
        ref[index, 16 * place : 16 * place + 16, lane : lane + 128] = part


def kernel(
    nx, ny, nz,
    px, pbc, pld, bx, bbc, bld, bprompt, blen,
    py, by,
    xall, inner, lead, outs, scores, c_cols, b_pad, run_cols, q_rows, w_rows, e_rows,
    state_parts, mid_parts, start_parts,
    ysend, yrecv, back, decay, xsend, xrecv, before, final, hub_state, tile, prompts, staged, start,
    in_sem, out_sem, ys, yr, xs, xr, bs, br, fs, fr, ts, tr, gs, gr,
):
    x, y, p = lax.axis_index("ctx_0"), lax.axis_index("ctx_1"), lax.axis_index("pair")
    hub = (x * ny + y) // 2
    is_hub = p == hub
    not_hub = p != hub

    barrier = pltpu.get_barrier_semaphore()

    def greet(where):
        pl.semaphore_signal(barrier, inc=1, device_id=where, device_id_type=MESH)

    for k in range(1, ny):
        greet({"ctx_1": lax.rem(y + k, ny)})
    for k in range(1, nx):
        greet({"ctx_0": lax.rem(x + k, nx)})

    @pl.when(is_hub)
    def _():
        for k in range(1, nz):
            greet({"pair": lax.rem(p + k, nz)})

    @pl.when(not_hub)
    def _():
        greet({"pair": hub})

    def x_copy(u):
        if u < 4:
            source = px.at[u // 2, :, pl.ds(512 * (u % 2), 512)]
        else:
            source = bx.at[(u - 4) // 2, pl.ds(BLOCK * (u % 2), BLOCK), :]
        return pltpu.make_async_copy(source, xall.at[u], in_sem.at[u])

    for u in range(8):
        x_copy(u).start()

    low8 = iota((8, 128), 1) < 64

    rows = jnp.concatenate([pld[0], pld[1]], axis=0)
    run = running_sums(rows)
    q = run - log_gain(rows)
    run_end = run[:, BLOCK - 1 : BLOCK]
    weights = jnp.exp2(run_end - q)
    ends = jnp.broadcast_to(jnp.exp2(run_end), (32, 128))
    q_rows[0:32, :] = q
    for u in range(4):
        x_copy(u).wait()
    for pr in range(2):
        b_rows = pbc[0, pr].astype(F32)
        states = pair_states(
            b_rows,
            weights[16 * pr : 16 * pr + 16],
            xall,
            lambda group, pr=pr: (2 * pr + group // 2, 256 * (group % 2)),
            16,
        )
        for j in range(8):
            ysend[j, 16 * pr : 16 * pr + 16, :] = states[j]
    first_row = iota((8, 128), 0) == 0
    for j in range(8):
        per_prompt = [
            pair_of(
                jnp.broadcast_to(ends[16 * pr + 2 * j : 16 * pr + 2 * j + 1], (8, 128)),
                jnp.broadcast_to(ends[16 * pr + 2 * j + 1 : 16 * pr + 2 * j + 2], (8, 128)),
                low8,
            )
            for pr in range(2)
        ]
        ysend[j, 32:40, :] = jnp.where(first_row, per_prompt[0], per_prompt[1])
    tile[...] = jnp.full((8, 128), bprompt[0], jnp.int32).astype(F32)

    pl.semaphore_wait(barrier, ny - 1 + nx - 1 + 1 + (nz - 2) * is_hub.astype(jnp.int32))

    def y_copy(k):
        there = lax.rem(y + k, ny)
        return pltpu.make_async_remote_copy(
            src_ref=ysend.at[there], dst_ref=yrecv.at[k], send_sem=ys.at[k], recv_sem=yr.at[k],
            device_id={"ctx_1": there}, device_id_type=MESH,
        )

    for k in far_first(ny):
        y_copy(k).start()

    from_hub = lax.rem(p - hub + nz, nz)

    def tile_copy(k):
        return pltpu.make_async_remote_copy(
            src_ref=tile, dst_ref=prompts.at[k], send_sem=ts, recv_sem=tr.at[k],
            device_id={"pair": hub}, device_id_type=MESH,
        )

    @pl.when(not_hub)
    def _():
        tile_copy(from_hub).start()

    yrecv[0] = ysend[y]

    b_rows_in = [bld[b, :, BLOCK * k : BLOCK * k + BLOCK] for b in range(2) for k in range(2)]
    rows = jnp.concatenate(b_rows_in, axis=0)
    b_run = running_sums(rows)
    b_q = b_run - log_gain(rows)
    b_end = b_run[:, BLOCK - 1 : BLOCK]
    q_rows[32:64, :] = b_q
    w_rows[...] = jnp.exp2(b_end - b_q)
    e_rows[...] = jnp.broadcast_to(jnp.exp2(b_end), (32, 128))
    run_cols[...] = jnp.concatenate([run, b_run, jnp.zeros((64, BLOCK), F32)], axis=0).T
    for s in range(6):
        if s < 2:
            b_in, c_in = pbc[0, s], pbc[1, s]
        else:
            b, k = (s - 2) // 2, s % 2
            b_in = bbc[0, b, :, BLOCK * k : BLOCK * k + BLOCK]
            c_in = bbc[1, b, :, BLOCK * k : BLOCK * k + BLOCK]
        c_in = c_in.astype(F32)
        c_cols[s] = jnp.concatenate([c_in, c_in, c_in, jnp.zeros((80, BLOCK), F32)], axis=0).T.astype(BF16)
        b_pad[s, 0:16, :] = b_in
        b_pad[s, 16:128, :] = jnp.zeros((112, BLOCK), BF16)
    for ref in (state_parts, mid_parts, start_parts):
        for i in range(ref.shape[0]):
            ref[i, 48:128, :] = jnp.zeros((80, 512), BF16)

    low256 = iota((BLOCK, 128), 1) < 64
    causal = iota((BLOCK, BLOCK), 1) <= iota((BLOCK, BLOCK), 0)

    def unit_pass(u, carry):
        s = jnp.where(u < 4, u // 2, u - 2)
        scores[...] = jnp.where(causal, dot(c_cols[s], b_pad[s]), 0.0)
        cols = pltpu.roll(run_cols[...], lax.rem(128 - 8 * u, 128), 1)
        q_unit = q_rows[pl.ds(pl.multiple_of(8 * u, 8), 8), :]
        for j in range(4):
            x_pair = xall[u, :, 128 * j : 128 * j + 128]
            products, spread = [], []
            for h in (2 * j, 2 * j + 1):
                col = jnp.broadcast_to(cols[:, h : h + 1], (BLOCK, 128))
                row = q_unit[h : h + 1, :]
                upper = jnp.exp2(jnp.minimum(col[:128] - row[:, :128], 0.0)) * scores[0:128, 0:128]
                left = jnp.exp2(jnp.minimum(col[128:] - row[:, :128], 0.0)) * scores[128:256, 0:128]
                right = jnp.exp2(jnp.minimum(col[128:] - row[:, 128:], 0.0)) * scores[128:256, 128:256]
                top = dot(upper.astype(BF16), x_pair[:128])
                low = dot(jnp.concatenate([left, right], axis=1).astype(BF16), x_pair)
                products.append(jnp.concatenate([top, low], axis=0))
                spread.append(col)
            inner[u, :, 128 * j : 128 * j + 128] = pair_of(products[0], products[1], low256)
            lead[u, :, 128 * j : 128 * j + 128] = jnp.exp2(pair_of(spread[0], spread[1], low256))
        return carry

    lax.fori_loop(0, 4, unit_pass, 0)

    for k in range(1, ny):
        y_copy(k).wait_recv()
    state = jnp.zeros((32, 128), F32)
    fall = jnp.ones((8, 128), F32)
    for s in range(ny):
        slot = lax.rem(y - s + ny, ny)
        back[s] = state
        decay[s] = fall
        step = yrecv[slot, 32:40, :]
        state = rows16(step) * state + yrecv[slot, 0:32, :]
        fall = fall * step
    xsend[0:32, :] = state
    xsend[32:40, :] = fall

    def x_row_copy(k):
        there = lax.rem(x + k, nx)
        return pltpu.make_async_remote_copy(
            src_ref=xsend, dst_ref=xrecv.at[k], send_sem=xs.at[k], recv_sem=xr.at[k],
            device_id={"ctx_0": there}, device_id_type=MESH,
        )

    for k in far_first(nx):
        x_row_copy(k).start()
    xrecv[0] = xsend[...]

    for u in range(4, 8):
        x_copy(u).wait()
    lax.fori_loop(4, 6, unit_pass, 0)

    for k in range(1, nx):
        x_row_copy(k).wait_recv()
    state = jnp.zeros((32, 128), F32)
    mine = state
    for s in range(nx):
        slot = lax.rem(x - s + nx, nx)
        mine = jnp.where(x == s, state, mine)
        state = rows16(xrecv[slot, 32:40, :]) * state + xrecv[slot, 0:32, :]
    final[...] = state

    hub_y = lax.rem(2 * p + y // 4, ny)
    place = lax.rem(y, 4)
    sends_final = x == (2 * p) // ny

    def final_copy():
        return pltpu.make_async_remote_copy(
            src_ref=final, dst_ref=hub_state.at[place], send_sem=fs, recv_sem=fr.at[place],
            device_id={"ctx_1": hub_y}, device_id_type=MESH,
        )

    @pl.when(jnp.logical_and(sends_final, y != hub_y))
    def _():
        final_copy().start()

    @pl.when(jnp.logical_and(sends_final, y == hub_y))
    def _():
        pltpu.make_async_copy(final, hub_state.at[place], fr.at[place]).start()

    def back_copy(k):
        there = lax.rem(y + k, ny)
        return pltpu.make_async_remote_copy(
            src_ref=back.at[there], dst_ref=before.at[k], send_sem=bs.at[k], recv_sem=br.at[k],
            device_id={"ctx_1": there}, device_id_type=MESH,
        )

    for s in range(ny):
        back[s] = back[s] + rows16(decay[s]) * mine
    for k in far_first(ny):
        back_copy(k).start()
    before[0] = back[y]

    lax.fori_loop(6, 8, unit_pass, 0)

    def start_copy(k):
        there = lax.rem(p + k, nz)
        return pltpu.make_async_remote_copy(
            src_ref=staged.at[k], dst_ref=start, send_sem=gs.at[k], recv_sem=gr,
            device_id={"pair": there}, device_id_type=MESH,
        )

    @pl.when(is_hub)
    def _():
        for i in range(4):
            pltpu.make_async_copy(final, hub_state.at[i], fr.at[i]).wait()
        for k in range(1, nz):
            tile_copy(k).wait_recv()
        for k in far_first(nz):
            first = prompts[k] < 0.5
            first = jnp.concatenate([first, first], axis=0)
            for i in range(4):
                staged[k, 16 * i : 16 * i + 16, :] = jnp.where(
                    first, hub_state[i, 0:16, :], hub_state[i, 16:32, :]
                )
            start_copy(k).start()
        first = tile[...] < 0.5
        first = jnp.concatenate([first, first], axis=0)
        for i in range(4):
            start[16 * i : 16 * i + 16, :] = jnp.where(
                first, hub_state[i, 0:16, :], hub_state[i, 16:32, :]
            )

    low1 = iota((1, 128), 1) < 64
    for b in range(2):
        first, second = 4 + 2 * b, 5 + 2 * b
        states = pair_states(
            bbc[0, b, :, 0:BLOCK].astype(F32),
            w_rows[16 * b : 16 * b + 8],
            xall,
            lambda group, first=first: (first, 256 * group),
            8,
        )
        for j in range(4):
            store_parts(mid_parts, b, 128 * j, states[j])
        carried = dot(c_cols[3 + 2 * b], mid_parts[b])
        place_of = iota((BLOCK, 128), 0)
        for j in range(4):
            lanes = slice(128 * j, 128 * j + 128)
            fall = pair_of(e_rows[16 * b + 2 * j : 16 * b + 2 * j + 1], e_rows[16 * b + 2 * j + 1 : 16 * b + 2 * j + 2], low1)
            live = place_of < blen[b]
            inner[first, :, lanes] = jnp.where(live, inner[first, :, lanes], 0.0)
            lead[first, :, lanes] = jnp.where(live, lead[first, :, lanes], 0.0)
            live = place_of + BLOCK < blen[b]
            own = lead[second, :, lanes]
            inner[second, :, lanes] = jnp.where(live, inner[second, :, lanes] + own * carried[:, lanes], 0.0)
            lead[second, :, lanes] = jnp.where(live, own * fall, 0.0)

    def finish(u, parts):
        s = u // 2 if u < 4 else u - 2
        carried = dot(c_cols[s], parts)
        outs[u] = (inner[u] + lead[u] * carried).astype(BF16)
        out_copy(u).start()

    def out_copy(u):
        if u < 4:
            target = py.at[u // 2, :, pl.ds(512 * (u % 2), 512)]
        else:
            target = by.at[(u - 4) // 2, pl.ds(BLOCK * (u % 2), BLOCK), :]
        return pltpu.make_async_copy(outs.at[u], target, out_sem.at[u])

    for k in range(1, ny):
        back_copy(k).wait_recv()
    for j in range(8):
        slot = lax.rem(y - j + ny, ny)
        for pr in range(2):
            store_parts(state_parts, 2 * pr + j // 4, 128 * (j % 4), before[slot, 16 * pr : 16 * pr + 16, :])
    for u in range(4):
        finish(u, state_parts[u])

    @pl.when(not_hub)
    def _():
        start_copy(1).wait_recv()

    for i in range(4):
        store_parts(start_parts, 0, 128 * i, start[16 * i : 16 * i + 16, :])
    for u in range(4, 8):
        finish(u, start_parts[0])

    for k in range(1, ny):
        y_copy(k).wait_send()
        back_copy(k).wait_send()
    for k in range(1, nx):
        x_row_copy(k).wait_send()

    @pl.when(jnp.logical_and(sends_final, y != hub_y))
    def _():
        final_copy().wait_send()

    @pl.when(not_hub)
    def _():
        tile_copy(from_hub).wait_send()

    @pl.when(is_hub)
    def _():
        for k in range(1, nz):
            start_copy(k).wait_send()

    for u in range(8):
        out_copy(u).wait()


def body(nx, ny, nz, px, pbc, pld, bx, bbc, bld, bprompt, blen):
    any_space = pl.BlockSpec(memory_space=pl.ANY)
    vmem = pl.BlockSpec(memory_space=pltpu.VMEM)
    smem = pl.BlockSpec(memory_space=pltpu.SMEM)
    dma = pltpu.SemaphoreType.DMA
    return pl.pallas_call(
        functools.partial(kernel, nx, ny, nz),
        out_shape=(jax.ShapeDtypeStruct(px.shape, BF16), jax.ShapeDtypeStruct(bx.shape, BF16)),
        in_specs=[any_space, vmem, vmem, any_space, vmem, vmem, smem, smem],
        out_specs=(any_space, any_space),
        scratch_shapes=[
            pltpu.VMEM((8, BLOCK, 512), BF16),
            pltpu.VMEM((8, BLOCK, 512), F32),
            pltpu.VMEM((8, BLOCK, 512), F32),
            pltpu.VMEM((8, BLOCK, 512), BF16),
            pltpu.VMEM((BLOCK, BLOCK), F32),
            pltpu.VMEM((6, BLOCK, 128), BF16),
            pltpu.VMEM((6, 128, BLOCK), BF16),
            pltpu.VMEM((BLOCK, 128), F32),
            pltpu.VMEM((64, BLOCK), F32),
            pltpu.VMEM((32, BLOCK), F32),
            pltpu.VMEM((32, 128), F32),
            pltpu.VMEM((4, 128, 512), BF16),
            pltpu.VMEM((2, 128, 512), BF16),
            pltpu.VMEM((1, 128, 512), BF16),
            pltpu.VMEM((ny, 40, 128), F32),
            pltpu.VMEM((ny, 40, 128), F32),
            pltpu.VMEM((ny, 32, 128), F32),
            pltpu.VMEM((ny, 8, 128), F32),
            pltpu.VMEM((40, 128), F32),
            pltpu.VMEM((nx, 40, 128), F32),
            pltpu.VMEM((ny, 32, 128), F32),
            pltpu.VMEM((32, 128), F32),
            pltpu.VMEM((4, 32, 128), F32),
            pltpu.VMEM((8, 128), F32),
            pltpu.VMEM((nz, 8, 128), F32),
            pltpu.VMEM((nz, 64, 128), F32),
            pltpu.VMEM((64, 128), F32),
            dma((8,)), dma((8,)),
            dma((ny,)), dma((ny,)),
            dma((nx,)), dma((nx,)),
            dma((ny,)), dma((ny,)),
            dma, dma((4,)),
            dma, dma((nz,)),
            dma((nz,)), dma,
        ],
        compiler_params=pltpu.CompilerParams(collective_id=0, has_side_effects=True),
        name="layer",
    )(px, pbc, pld, bx, bbc, bld, bprompt, blen)


def solution(mesh):
    nx = 4
    ny, nz = mesh.shape["ctx"] // nx, mesh.shape["pair"]
    finer = Mesh(mesh.devices.reshape(nx, ny, nz), ("ctx_0", "ctx_1", "pair"))
    return jax.shard_map(
        functools.partial(body, nx, ny, nz),
        mesh=finer,
        in_specs=(
            P(None, CTX, "pair"),
            P(None, None, None, CTX),
            P(None, "pair", CTX),
            P("pair", None, CTX),
            P(None, "pair", None, None),
            P("pair", CTX, None),
            P("pair"),
            P("pair"),
        ),
        out_specs=(P(None, CTX, "pair"), P("pair", None, CTX)),
        check_vma=False,
    )
```

```python
import functools

import jax
import jax.numpy as jnp
from jax import lax
from jax.experimental import pallas as pl
from jax.experimental.pallas import tpu as pltpu
from jax.sharding import Mesh
from jax.sharding import PartitionSpec as P

MESH = pl.DeviceIdType.MESH
CTX = ("ctx_0", "ctx_1")
F32 = jnp.float32
BF16 = jnp.bfloat16
BLOCK = 256
LOG2E = 1.4426950408889634
FIRST_PART = 6
SECOND_PART = 8


def iota(shape, dim):
    return lax.broadcasted_iota(jnp.int32, shape, dim)


def dot(a, b):
    return jnp.dot(a, b, preferred_element_type=F32)


def far_first(n):
    return sorted(range(1, n), key=lambda k: -min(k, n - k))


def three_parts(a):
    hi = a.astype(BF16)
    rest = a - hi.astype(F32)
    mid = rest.astype(BF16)
    low = (rest - mid.astype(F32)).astype(BF16)
    return hi, mid, low


def running_sums(rows):
    until = (iota((BLOCK, BLOCK), 0) <= iota((BLOCK, BLOCK), 1)).astype(F32).astype(BF16)
    count = rows.shape[0]
    sums = dot(jnp.concatenate(three_parts(rows), axis=0), until)
    total = sums[:count] + (sums[count : 2 * count] + sums[2 * count :])
    return total * LOG2E


def log_gain(rows):
    z = 2.0 * rows
    series = 1.0 / 362880.0
    for factor in (40320.0, 5040.0, 720.0, 120.0, 24.0, 6.0, 2.0, 1.0):
        series = series * z + 1.0 / factor
    squared = jnp.where(z > -0.5, -z * series, 1.0 - jnp.exp(z))
    return jnp.where(squared > 0.0, (0.5 * LOG2E) * jnp.log(squared), -1e30)


def pair_of(even, odd, low_lanes):
    return jnp.where(low_lanes, even, odd)


def rows16(tile):
    return jnp.concatenate(
        [jnp.broadcast_to(tile[0:1], (16, 128)), jnp.broadcast_to(tile[1:2], (16, 128))], axis=0
    )


def pair_states(b_rows, weights, x_ref, unit_of, heads):
    low16 = iota((16, 128), 1) < 64
    found = []
    for group in range(heads // 4):
        push = jnp.concatenate(
            [b_rows * weights[4 * group + i : 4 * group + i + 1, :] for i in range(4)], axis=0
        ).astype(BF16)
        unit, lane = unit_of(group)
        sums = dot(push, x_ref[unit, :, lane : lane + 256])
        for i in range(2):
            part = sums[32 * i : 32 * i + 32, 128 * i : 128 * i + 128]
            found.append(pair_of(part[0:16], part[16:32], low16))
    return found


def store_parts(ref, lane, state):
    for place, part in enumerate(three_parts(state)):
        ref[16 * place : 16 * place + 16, lane : lane + 128] = part


def kernel(
    nx, ny, nz,
    px, pbc_in, pld_in, bx, bbc_in, bld_in, blen_in, bprompt,
    prompt_outs, b_inner, b_lead, start_parts, b_cols,
    pbc, pld, bbc, bld, blen,
    xall, p_inner, p_lead, scores, c_cols, b_pad, run_cols, q_rows, w_rows, e_rows,
    state_parts, mid_parts,
    ysend, yfall, yrecv, yfell, back, decay, xsend, xfall, xrecv, xfell, before, row_in, row_fell,
    tile, prompts, staged, start,
    in_sem, ys, yr, ds, dr, xs, xr, es, er, bs, br, fs, fr, ts, tr, gs, gr,
):
    x, y, p = lax.axis_index("ctx_0"), lax.axis_index("ctx_1"), lax.axis_index("pair")
    hub = (x * ny + y) // 2
    is_hub = p == hub
    not_hub = p != hub

    barrier = pltpu.get_barrier_semaphore()

    def greet(where):
        pl.semaphore_signal(barrier, inc=1, device_id=where, device_id_type=MESH)

    first_hub = lax.rem(2 * p, ny)

    def holder(j):
        return lax.rem(first_hub + ny + (j - 3 if j >= 4 else -j), ny)

    def held_by(at):
        far = lax.rem(at - first_hub + ny, ny)
        return jnp.where(jnp.logical_and(far >= 1, far <= 4), far + 3, lax.rem(ny - far, ny))

    mine_j = held_by(y)
    place = lax.rem(mine_j, 4)
    hub_x = (2 * p) // ny
    hub_y = lax.rem(first_hub + mine_j // 4, ny)
    other_row = x != hub_x
    at_hub = jnp.logical_and(x == hub_x, y == hub_y)
    from_hub = jnp.logical_not(at_hub)
    for k in range(1, ny):
        greet({"ctx_1": lax.rem(y + k, ny)})
    for k in range(1, nx):
        greet({"ctx_0": lax.rem(x + k, nx)})

    @pl.when(is_hub)
    def _():
        for k in range(1, nz):
            greet({"pair": lax.rem(p + k, nz)})
        side = 2 * (y - first_hub) - 1
        for k in range(1, nx):
            for i in range(4):
                greet({"ctx_0": lax.rem(x + k, nx), "ctx_1": lax.rem(y + side * i + ny, ny)})

    @pl.when(other_row)
    def _():
        greet({"ctx_0": hub_x, "ctx_1": hub_y})

    @pl.when(not_hub)
    def _():
        greet({"pair": hub})

    small = [
        pltpu.make_async_copy(source, target, in_sem.at[8 + i])
        for i, (source, target) in enumerate(
            [(pld_in, pld), (pbc_in, pbc), (bld_in, bld), (bbc_in, bbc), (blen_in, blen)]
        )
    ]

    def x_copy(u):
        if u < 4:
            source = px.at[u // 2, :, pl.ds(512 * (u % 2), 512)]
        else:
            source = bx.at[(u - 4) // 2, pl.ds(BLOCK * (u % 2), BLOCK), :]
        return pltpu.make_async_copy(source, xall.at[u], in_sem.at[u])

    small[0].start()
    small[1].start()
    for u in range(4):
        x_copy(u).start()
    for copy in small[2:]:
        copy.start()
    for u in range(4, 8):
        x_copy(u).start()

    def y_copy(pr, k):
        there = lax.rem(y + k, ny)
        return pltpu.make_async_remote_copy(
            src_ref=ysend.at[pr, held_by(there)], dst_ref=yrecv.at[pr, k],
            send_sem=ys.at[ny * pr + k], recv_sem=yr.at[ny * pr + k],
            device_id={"ctx_1": there}, device_id_type=MESH,
        )

    def fall_copy(k):
        there = lax.rem(y + k, ny)
        return pltpu.make_async_remote_copy(
            src_ref=yfall.at[held_by(there)], dst_ref=yfell.at[k], send_sem=ds.at[k], recv_sem=dr.at[k],
            device_id={"ctx_1": there}, device_id_type=MESH,
        )

    def tile_copy(of):
        return pltpu.make_async_remote_copy(
            src_ref=tile, dst_ref=prompts.at[of], send_sem=ts, recv_sem=tr.at[of],
            device_id={"pair": hub}, device_id_type=MESH,
        )

    low8 = iota((8, 128), 1) < 64

    small[0].wait()
    rows = jnp.concatenate([pld[0], pld[1]], axis=0)
    run = running_sums(rows)
    q = run - log_gain(rows)
    run_end = run[:, BLOCK - 1 : BLOCK]
    weights = jnp.exp2(run_end - q)
    ends = jnp.broadcast_to(jnp.exp2(run_end), (32, 128))
    q_rows[0:32, :] = q
    low1 = iota((1, 128), 1) < 64
    for pr in range(2):
        for j in range(8):
            h = 16 * pr + 2 * j
            yfall[j, pr : pr + 1, :] = pair_of(ends[h : h + 1], ends[h + 1 : h + 2], low1)
    small[1].wait()
    for pr in range(2):
        x_copy(2 * pr).wait()
        x_copy(2 * pr + 1).wait()
        states = pair_states(
            pbc[0, pr].astype(F32),
            weights[16 * pr : 16 * pr + 16],
            xall,
            lambda group, pr=pr: (2 * pr + group // 2, 256 * (group % 2)),
            16,
        )
        for j in range(8):
            ysend[pr, j] = states[j]
        if pr == 0:
            more = (nz - 2 + 4 * (nx - 1)) * is_hub.astype(jnp.int32) + other_row.astype(jnp.int32)
            pl.semaphore_wait(barrier, ny - 1 + nx - 1 + 1 + more)
        for k in far_first(ny):
            y_copy(pr, k).start()
    for k in far_first(ny):
        fall_copy(k).start()
    tile[...] = jnp.full((8, 128), bprompt[0], jnp.int32).astype(F32)

    @pl.when(not_hub)
    def _():
        tile_copy(p).start()

    for pr in range(2):
        yrecv[pr, 0] = ysend[pr, mine_j]
    yfell[0] = yfall[mine_j]

    small[2].wait()
    small[3].wait()
    b_rows_in = [bld[b, :, BLOCK * k : BLOCK * k + BLOCK] for b in range(2) for k in range(2)]
    rows = jnp.concatenate(b_rows_in, axis=0)
    b_run = running_sums(rows)
    b_q = b_run - log_gain(rows)
    b_end = b_run[:, BLOCK - 1 : BLOCK]
    q_rows[32:64, :] = b_q
    w_rows[...] = jnp.exp2(b_end - b_q)
    e_rows[...] = jnp.broadcast_to(jnp.exp2(b_end), (32, 128))
    run_cols[...] = jnp.concatenate([run, b_run, jnp.zeros((64, BLOCK), F32)], axis=0).T
    for s in range(6):
        if s < 2:
            b_in, c_in = pbc[0, s], pbc[1, s]
        else:
            b, k = (s - 2) // 2, s % 2
            b_in = bbc[0, b, :, BLOCK * k : BLOCK * k + BLOCK]
            c_in = bbc[1, b, :, BLOCK * k : BLOCK * k + BLOCK]
        c_in = c_in.astype(F32)
        cols = jnp.concatenate([c_in, c_in, c_in, jnp.zeros((80, BLOCK), F32)], axis=0).T.astype(BF16)
        c_cols[s] = cols
        if s >= 2:
            b_cols[s - 2] = cols
        b_pad[s, 0:16, :] = b_in
        b_pad[s, 16:128, :] = jnp.zeros((112, BLOCK), BF16)
    start_parts[48:128, :] = jnp.zeros((80, 512), BF16)
    for ref in (state_parts, mid_parts):
        for i in range(ref.shape[0]):
            ref[i, 48:128, :] = jnp.zeros((80, 512), BF16)

    low256 = iota((BLOCK, 128), 1) < 64
    causal = iota((BLOCK, BLOCK), 1) <= iota((BLOCK, BLOCK), 0)

    def unit_pass(inner, lead, base, u, carry):
        s = jnp.where(u < 4, u // 2, u - 2)
        scores[...] = jnp.where(causal, dot(c_cols[s], b_pad[s]), 0.0)
        cols = pltpu.roll(run_cols[...], lax.rem(128 - 8 * u, 128), 1)
        q_unit = q_rows[pl.ds(pl.multiple_of(8 * u, 8), 8), :]
        for j in range(4):
            x_pair = xall[u, :, 128 * j : 128 * j + 128]
            products, spread = [], []
            for h in (2 * j, 2 * j + 1):
                col = jnp.broadcast_to(cols[:, h : h + 1], (BLOCK, 128))
                row = q_unit[h : h + 1, :]
                upper = jnp.exp2(jnp.minimum(col[:128] - row[:, :128], 0.0)) * scores[0:128, 0:128]
                left = jnp.exp2(jnp.minimum(col[128:] - row[:, :128], 0.0)) * scores[128:256, 0:128]
                right = jnp.exp2(jnp.minimum(col[128:] - row[:, 128:], 0.0)) * scores[128:256, 128:256]
                top = dot(upper.astype(BF16), x_pair[:128])
                low = dot(jnp.concatenate([left, right], axis=1).astype(BF16), x_pair)
                products.append(jnp.concatenate([top, low], axis=0))
                spread.append(col)
            inner[u - base, :, 128 * j : 128 * j + 128] = pair_of(products[0], products[1], low256)
            lead[u - base, :, 128 * j : 128 * j + 128] = jnp.exp2(pair_of(spread[0], spread[1], low256))
        return carry

    b_pass = functools.partial(unit_pass, b_inner, b_lead, 4)
    lax.fori_loop(0, 4, functools.partial(unit_pass, p_inner, p_lead, 0), 0)
    for u in range(4, 8):
        x_copy(u).wait()
    lax.fori_loop(4, FIRST_PART, b_pass, 0)

    for k in range(1, ny):
        fall_copy(k).wait_recv()
        for pr in range(2):
            y_copy(pr, k).wait_recv()
    state = [jnp.zeros((16, 128), F32)] * 2
    fall = jnp.ones((2, 128), F32)
    for s in range(ny):
        slot = lax.rem(y - s + ny, ny)
        decay[s] = fall
        step = yfell[slot]
        for pr in range(2):
            back[s, 16 * pr : 16 * pr + 16, :] = state[pr]
            state[pr] = step[pr : pr + 1] * state[pr] + yrecv[pr, slot]
        fall = fall * step
    for pr in range(2):
        xsend[16 * pr : 16 * pr + 16, :] = state[pr]
    xfall[...] = fall

    def x_row_copy(k):
        there = lax.rem(x + k, nx)
        return pltpu.make_async_remote_copy(
            src_ref=xsend, dst_ref=xrecv.at[k], send_sem=xs.at[k], recv_sem=xr.at[k],
            device_id={"ctx_0": there}, device_id_type=MESH,
        )

    def x_fall_copy(k):
        there = lax.rem(x + k, nx)
        return pltpu.make_async_remote_copy(
            src_ref=xfall, dst_ref=xfell.at[k], send_sem=es.at[k], recv_sem=er.at[k],
            device_id={"ctx_0": there}, device_id_type=MESH,
        )

    def total_copy():
        return pltpu.make_async_remote_copy(
            src_ref=xsend, dst_ref=row_in.at[x, place], send_sem=fs.at[0], recv_sem=fr.at[0, 4 * x + place],
            device_id={"ctx_0": hub_x, "ctx_1": hub_y}, device_id_type=MESH,
        )

    def total_fall_copy():
        return pltpu.make_async_remote_copy(
            src_ref=xfall, dst_ref=row_fell.at[x, place], send_sem=fs.at[1], recv_sem=fr.at[1, 4 * x + place],
            device_id={"ctx_0": hub_x, "ctx_1": hub_y}, device_id_type=MESH,
        )

    @pl.when(from_hub)
    def _():
        total_copy().start()
        total_fall_copy().start()

    @pl.when(at_hub)
    def _():
        pltpu.make_async_copy(xsend, row_in.at[x, place], fr.at[0, 4 * x + place]).start()
        pltpu.make_async_copy(xfall, row_fell.at[x, place], fr.at[1, 4 * x + place]).start()

    for k in far_first(nx):
        x_row_copy(k).start()
        x_fall_copy(k).start()
    xrecv[0] = xsend[...]
    xfell[0] = xfall[...]

    lax.fori_loop(FIRST_PART, SECOND_PART, b_pass, 0)

    for k in range(1, nx):
        x_fall_copy(k).wait_recv()
        x_row_copy(k).wait_recv()
    state = jnp.zeros((32, 128), F32)
    mine = state
    for s in range(nx):
        mine = jnp.where(x == s, state, mine)
        if s < nx - 1:
            slot = lax.rem(x - s + nx, nx)
            state = rows16(xfell[slot]) * state + xrecv[slot]

    def back_copy(k):
        there = lax.rem(y + k, ny)
        return pltpu.make_async_remote_copy(
            src_ref=back.at[there], dst_ref=before.at[k], send_sem=bs.at[k], recv_sem=br.at[k],
            device_id={"ctx_1": there}, device_id_type=MESH,
        )

    for s in range(ny):
        back[s] = back[s] + rows16(decay[s]) * mine
    for k in far_first(ny):
        back_copy(k).start()
    before[0] = back[y]

    lax.fori_loop(SECOND_PART, 8, b_pass, 0)

    def start_copy(to):
        return pltpu.make_async_remote_copy(
            src_ref=staged.at[to], dst_ref=start, send_sem=gs.at[to], recv_sem=gr,
            device_id={"pair": to}, device_id_type=MESH,
        )

    def chosen(flags, states):
        first = jnp.concatenate([flags, flags], axis=0) < 0.5
        return [jnp.where(first, state[0:16], state[16:32]) for state in states]

    @pl.when(is_hub)
    def _():
        states = []
        for i in range(4):
            state = jnp.zeros((32, 128), F32)
            for s in range(nx):
                pltpu.make_async_copy(xsend, row_in.at[s, i], fr.at[0, 4 * s + i]).wait()
                pltpu.make_async_copy(xfall, row_fell.at[s, i], fr.at[1, 4 * s + i]).wait()
                state = rows16(row_fell[s, i]) * state + row_in[s, i]
            states.append(state)
        for to in range(nz):

            @pl.when(p != to)
            def _(to=to):
                tile_copy(to).wait_recv()
                for i, state in enumerate(chosen(prompts[to], states)):
                    staged[to, 16 * i : 16 * i + 16, :] = state
                start_copy(to).start()

        for i, state in enumerate(chosen(tile[...], states)):
            start[16 * i : 16 * i + 16, :] = state

    small[4].wait()
    for b in range(2):
        first, second = 2 * b, 2 * b + 1
        states = pair_states(
            bbc[0, b, :, 0:BLOCK].astype(F32),
            w_rows[16 * b : 16 * b + 8],
            xall,
            lambda group, b=b: (4 + 2 * b, 256 * group),
            8,
        )
        for j in range(4):
            store_parts(mid_parts.at[b], 128 * j, states[j])
        carried = dot(c_cols[3 + 2 * b], mid_parts[b])
        place_of = iota((BLOCK, 128), 0)
        for j in range(4):
            lanes = slice(128 * j, 128 * j + 128)
            fall = pair_of(e_rows[16 * b + 2 * j : 16 * b + 2 * j + 1], e_rows[16 * b + 2 * j + 1 : 16 * b + 2 * j + 2], low1)
            live = place_of < blen[b]
            b_inner[first, :, lanes] = jnp.where(live, b_inner[first, :, lanes], 0.0)
            b_lead[first, :, lanes] = jnp.where(live, b_lead[first, :, lanes], 0.0)
            live = place_of + BLOCK < blen[b]
            own = b_lead[second, :, lanes]
            b_inner[second, :, lanes] = jnp.where(live, b_inner[second, :, lanes] + own * carried[:, lanes], 0.0)
            b_lead[second, :, lanes] = jnp.where(live, own * fall, 0.0)

    for k in range(1, ny):
        back_copy(k).wait_recv()
    for j in range(8):
        slot = lax.rem(y - holder(j) + ny, ny)
        for pr in range(2):
            store_parts(
                state_parts.at[2 * pr + j // 4], 128 * (j % 4), before[slot, 16 * pr : 16 * pr + 16, :]
            )
    for u in range(4):
        carried = dot(c_cols[u // 2], state_parts[u])
        prompt_outs[u] = (p_inner[u] + p_lead[u] * carried).astype(BF16)

    for k in range(1, ny):
        for pr in range(2):
            y_copy(pr, k).wait_send()
        fall_copy(k).wait_send()
        back_copy(k).wait_send()
    for k in range(1, nx):
        x_row_copy(k).wait_send()
        x_fall_copy(k).wait_send()

    @pl.when(from_hub)
    def _():
        total_copy().wait_send()
        total_fall_copy().wait_send()

    @pl.when(not_hub)
    def _():
        tile_copy(p).wait_send()
        start_copy(0).wait_recv()

    for i in range(4):
        store_parts(start_parts, 128 * i, start[16 * i : 16 * i + 16, :])

    @pl.when(is_hub)
    def _():
        for to in range(nz):

            @pl.when(p != to)
            def _(to=to):
                start_copy(to).wait_send()


def write_kernel(prompt_outs, b_inner, b_lead, start_parts, b_cols, py, by, outs, sem):
    copies = [
        pltpu.make_async_copy(prompt_outs.at[u], py.at[u // 2, :, pl.ds(512 * (u % 2), 512)], sem.at[u])
        for u in range(4)
    ]
    for copy in copies:
        copy.start()
    for u in range(4):
        outs[u] = (b_inner[u] + b_lead[u] * dot(b_cols[u], start_parts[...])).astype(BF16)
        copy = pltpu.make_async_copy(
            outs.at[u], by.at[u // 2, pl.ds(BLOCK * (u % 2), BLOCK), :], sem.at[4 + u]
        )
        copy.start()
        copies.append(copy)
    for copy in copies:
        copy.wait()


def body(nx, ny, nz, px, pbc, pld, bx, bbc, bld, bprompt, blen):
    any_space = pl.BlockSpec(memory_space=pl.ANY)
    vmem = pl.BlockSpec(memory_space=pltpu.VMEM)
    dma = pltpu.SemaphoreType.DMA
    between = [
        pltpu.VMEM((4, BLOCK, 512), BF16),
        pltpu.VMEM((4, BLOCK, 512), F32),
        pltpu.VMEM((4, BLOCK, 512), F32),
        pltpu.VMEM((128, 512), BF16),
        pltpu.VMEM((4, BLOCK, 128), BF16),
    ]
    kept = pl.pallas_call(
        functools.partial(kernel, nx, ny, nz),
        out_shape=between,
        in_specs=[pl.BlockSpec(memory_space=pltpu.HBM)] * 7 + [pl.BlockSpec(memory_space=pltpu.SMEM)],
        out_specs=[vmem] * 5,
        scratch_shapes=[
            pltpu.VMEM(pbc.shape, BF16),
            pltpu.VMEM(pld.shape, F32),
            pltpu.VMEM(bbc.shape, BF16),
            pltpu.VMEM(bld.shape, F32),
            pltpu.SMEM(blen.shape, jnp.int32),
            pltpu.VMEM((8, BLOCK, 512), BF16),
            pltpu.VMEM((4, BLOCK, 512), F32),
            pltpu.VMEM((4, BLOCK, 512), F32),
            pltpu.VMEM((BLOCK, BLOCK), F32),
            pltpu.VMEM((6, BLOCK, 128), BF16),
            pltpu.VMEM((6, 128, BLOCK), BF16),
            pltpu.VMEM((BLOCK, 128), F32),
            pltpu.VMEM((64, BLOCK), F32),
            pltpu.VMEM((32, BLOCK), F32),
            pltpu.VMEM((32, 128), F32),
            pltpu.VMEM((4, 128, 512), BF16),
            pltpu.VMEM((2, 128, 512), BF16),
            pltpu.VMEM((2, ny, 16, 128), F32),
            pltpu.VMEM((ny, 2, 128), F32),
            pltpu.VMEM((2, ny, 16, 128), F32),
            pltpu.VMEM((ny, 2, 128), F32),
            pltpu.VMEM((ny, 32, 128), F32),
            pltpu.VMEM((ny, 2, 128), F32),
            pltpu.VMEM((32, 128), F32),
            pltpu.VMEM((2, 128), F32),
            pltpu.VMEM((nx, 32, 128), F32),
            pltpu.VMEM((nx, 2, 128), F32),
            pltpu.VMEM((ny, 32, 128), F32),
            pltpu.VMEM((nx, 4, 32, 128), F32),
            pltpu.VMEM((nx, 4, 2, 128), F32),
            pltpu.VMEM((8, 128), F32),
            pltpu.VMEM((nz, 8, 128), F32),
            pltpu.VMEM((nz, 64, 128), F32),
            pltpu.VMEM((64, 128), F32),
            dma((13,)),
            dma((2 * ny,)), dma((2 * ny,)),
            dma((ny,)), dma((ny,)),
            dma((nx,)), dma((nx,)),
            dma((nx,)), dma((nx,)),
            dma((ny,)), dma((ny,)),
            dma((2,)), dma((2, 4 * nx)),
            dma, dma((nz,)),
            dma((nz,)), dma,
        ],
        compiler_params=pltpu.CompilerParams(
            collective_id=0, has_side_effects=True, vmem_limit_bytes=40 * 1024 * 1024
        ),
        name="layer",
    )(*[pltpu.with_memory_space_constraint(a, pltpu.HBM) for a in (px, pbc, pld, bx, bbc, bld, blen)], bprompt)
    return pl.pallas_call(
        write_kernel,
        out_shape=(jax.ShapeDtypeStruct(px.shape, BF16), jax.ShapeDtypeStruct(bx.shape, BF16)),
        in_specs=[vmem] * 5,
        out_specs=(any_space, any_space),
        scratch_shapes=[pltpu.VMEM((4, BLOCK, 512), BF16), dma((8,))],
        compiler_params=pltpu.CompilerParams(vmem_limit_bytes=16 * 1024 * 1024),
        name="write",
    )(*kept)


def solution(mesh):
    nx = 4
    ny, nz = mesh.shape["ctx"] // nx, mesh.shape["pair"]
    finer = Mesh(mesh.devices.reshape(nx, ny, nz), ("ctx_0", "ctx_1", "pair"))
    return jax.shard_map(
        functools.partial(body, nx, ny, nz),
        mesh=finer,
        in_specs=(
            P(None, CTX, "pair"),
            P(None, None, None, CTX),
            P(None, "pair", CTX),
            P("pair", None, CTX),
            P(None, "pair", None, None),
            P("pair", CTX, None),
            P("pair"),
            P("pair"),
        ),
        out_specs=(P(None, CTX, "pair"), P("pair", None, CTX)),
        check_vma=False,
    )
```

```python
import functools

import jax
import jax.numpy as jnp
from jax import lax
from jax.experimental import pallas as pl
from jax.experimental.pallas import tpu as pltpu
from jax.sharding import Mesh
from jax.sharding import PartitionSpec as P

MESH = pl.DeviceIdType.MESH
CTX = ("ctx_0", "ctx_1")
F32 = jnp.float32
BF16 = jnp.bfloat16
BLOCK = 256
LOG2E = 1.4426950408889634


def iota(shape, dim):
    return lax.broadcasted_iota(jnp.int32, shape, dim)


def dot(a, b):
    return jnp.dot(a, b, preferred_element_type=F32)


def far_first(n):
    return sorted(range(1, n), key=lambda k: -min(k, n - k))


def three_parts(a):
    hi = a.astype(BF16)
    rest = a - hi.astype(F32)
    mid = rest.astype(BF16)
    low = (rest - mid.astype(F32)).astype(BF16)
    return hi, mid, low


def running_sums(rows):
    until = (iota((BLOCK, BLOCK), 0) <= iota((BLOCK, BLOCK), 1)).astype(F32).astype(BF16)
    count = rows.shape[0]
    sums = dot(jnp.concatenate(three_parts(rows), axis=0), until)
    total = sums[:count] + (sums[count : 2 * count] + sums[2 * count :])
    return total * LOG2E


def log_gain(rows):
    z = 2.0 * rows
    series = 1.0 / 362880.0
    for factor in (40320.0, 5040.0, 720.0, 120.0, 24.0, 6.0, 2.0, 1.0):
        series = series * z + 1.0 / factor
    squared = jnp.where(z > -0.5, -z * series, 1.0 - jnp.exp(z))
    return jnp.where(squared > 0.0, (0.5 * LOG2E) * jnp.log(squared), -1e30)


def pair_of(even, odd, low_lanes):
    return jnp.where(low_lanes, even, odd)


def rows16(tile):
    return jnp.concatenate(
        [jnp.broadcast_to(tile[0:1], (16, 128)), jnp.broadcast_to(tile[1:2], (16, 128))], axis=0
    )


def pair_states(b_rows, weights, x_ref, unit_of, heads):
    low16 = iota((16, 128), 1) < 64
    found = []
    for group in range(heads // 4):
        push = jnp.concatenate(
            [b_rows * weights[4 * group + i : 4 * group + i + 1, :] for i in range(4)], axis=0
        ).astype(BF16)
        unit, lane = unit_of(group)
        sums = dot(push, x_ref[unit, :, lane : lane + 256])
        for i in range(2):
            part = sums[32 * i : 32 * i + 32, 128 * i : 128 * i + 128]
            found.append(pair_of(part[0:16], part[16:32], low16))
    return found


def wait_for(ref, sem):
    pltpu.make_async_copy(ref, ref, sem).wait()


def store_parts(ref, lane, state):
    for place, part in enumerate(three_parts(state)):
        ref[16 * place : 16 * place + 16, lane : lane + 128] = part


def kernel(
    nx, ny, nz,
    px, pbc_in, pld_in, bx, bbc_in, bld_in, blen_in, bprompt,
    prompt_outs, b_inner, b_lead, start_parts, b_cols,
    pbc, pld, bbc, bld, blen,
    xall, p_inner, p_lead, scores, c_cols, b_pad, run_cols, q_rows, w_rows, e_rows,
    state_parts, mid_parts,
    ysend, yfall, yrecv, yfell, back, decay, xsend, xfall, xrecv, xfell, before, row_in, row_fell,
    tile, prompts, staged, start,
    in_sem, ys, yr, ds, dr, xs, xr, es, er, bs, br, fs, fr, ts, tr, gs, gr,
):
    x, y, p = lax.axis_index("ctx_0"), lax.axis_index("ctx_1"), lax.axis_index("pair")
    hub = (x * ny + y) // 2
    is_hub = p == hub
    not_hub = p != hub

    barrier = pltpu.get_barrier_semaphore()

    def greet(where):
        pl.semaphore_signal(barrier, inc=1, device_id=where, device_id_type=MESH)

    first_hub = lax.rem(2 * p, ny)

    def holder(j):
        return lax.rem(first_hub + ny + (j - 3 if j >= 4 else -j), ny)

    def held_by(at):
        far = lax.rem(at - first_hub + ny, ny)
        return jnp.where(jnp.logical_and(far >= 1, far <= 4), far + 3, lax.rem(ny - far, ny))

    mine_j = held_by(y)
    place = lax.rem(mine_j, 4)
    hub_x = (2 * p) // ny
    hub_y = lax.rem(first_hub + mine_j // 4, ny)
    other_row = x != hub_x
    at_hub = jnp.logical_and(x == hub_x, y == hub_y)
    from_hub = jnp.logical_not(at_hub)
    for k in range(1, ny):
        greet({"ctx_1": lax.rem(y + k, ny)})
    for k in range(1, nx):
        greet({"ctx_0": lax.rem(x + k, nx)})

    @pl.when(is_hub)
    def _():
        for k in range(1, nz):
            greet({"pair": lax.rem(p + k, nz)})
        side = 2 * (y - first_hub) - 1
        for k in range(1, nx):
            for i in range(4):
                greet({"ctx_0": lax.rem(x + k, nx), "ctx_1": lax.rem(y + side * i + ny, ny)})

    @pl.when(other_row)
    def _():
        greet({"ctx_0": hub_x, "ctx_1": hub_y})

    @pl.when(not_hub)
    def _():
        greet({"pair": hub})

    small = [
        pltpu.make_async_copy(source, target, in_sem.at[3 + i])
        for i, (source, target) in enumerate(
            [(pld_in, pld), (pbc_in, pbc), (bld_in, bld), (bbc_in, bbc), (blen_in, blen)]
        )
    ]

    def x_copy(u):
        if u < 4:
            source = px.at[u // 2, :, pl.ds(512 * (u % 2), 512)]
        else:
            source = bx.at[(u - 4) // 2, pl.ds(BLOCK * (u % 2), BLOCK), :]
        return pltpu.make_async_copy(source, xall.at[u], in_sem.at[min(u // 2, 2)])

    small[0].start()
    small[1].start()
    for u in range(4):
        x_copy(u).start()
    for copy in small[2:]:
        copy.start()
    for u in range(4, 8):
        x_copy(u).start()

    def y_copy(pr, k):
        there = lax.rem(y + k, ny)
        return pltpu.make_async_remote_copy(
            src_ref=ysend.at[pr, held_by(there)], dst_ref=yrecv.at[pr, k],
            send_sem=ys, recv_sem=yr,
            device_id={"ctx_1": there}, device_id_type=MESH,
        )

    def fall_copy(k):
        there = lax.rem(y + k, ny)
        return pltpu.make_async_remote_copy(
            src_ref=yfall.at[held_by(there)], dst_ref=yfell.at[k], send_sem=ds, recv_sem=dr,
            device_id={"ctx_1": there}, device_id_type=MESH,
        )

    def tile_copy(of):
        return pltpu.make_async_remote_copy(
            src_ref=tile, dst_ref=prompts.at[of], send_sem=ts, recv_sem=tr,
            device_id={"pair": hub}, device_id_type=MESH,
        )

    low8 = iota((8, 128), 1) < 64

    small[0].wait()
    rows = jnp.concatenate([pld[0], pld[1]], axis=0)
    run = running_sums(rows)
    q = run - log_gain(rows)
    run_end = run[:, BLOCK - 1 : BLOCK]
    weights = jnp.exp2(run_end - q)
    ends = jnp.broadcast_to(jnp.exp2(run_end), (32, 128))
    q_rows[0:32, :] = q
    low1 = iota((1, 128), 1) < 64
    for pr in range(2):
        for j in range(8):
            h = 16 * pr + 2 * j
            yfall[j, pr : pr + 1, :] = pair_of(ends[h : h + 1], ends[h + 1 : h + 2], low1)
    small[1].wait()
    for pr in range(2):
        wait_for(xall.at[pl.ds(2 * pr, 2)], in_sem.at[pr])
        states = pair_states(
            pbc[0, pr].astype(F32),
            weights[16 * pr : 16 * pr + 16],
            xall,
            lambda group, pr=pr: (2 * pr + group // 2, 256 * (group % 2)),
            16,
        )
        for j in range(8):
            ysend[pr, j] = states[j]
        if pr == 0:
            more = (nz - 2 + 4 * (nx - 1)) * is_hub.astype(jnp.int32) + other_row.astype(jnp.int32)
            pl.semaphore_wait(barrier, ny - 1 + nx - 1 + 1 + more)
        for k in far_first(ny):
            y_copy(pr, k).start()
    for k in far_first(ny):
        fall_copy(k).start()
    tile[...] = jnp.full((8, 128), bprompt[0], jnp.int32).astype(F32)

    @pl.when(not_hub)
    def _():
        tile_copy(p).start()

    for pr in range(2):
        yrecv[pr, 0] = ysend[pr, mine_j]
    yfell[0] = yfall[mine_j]

    small[2].wait()
    small[3].wait()
    b_rows_in = [bld[b, :, BLOCK * k : BLOCK * k + BLOCK] for b in range(2) for k in range(2)]
    rows = jnp.concatenate(b_rows_in, axis=0)
    b_run = running_sums(rows)
    b_q = b_run - log_gain(rows)
    b_end = b_run[:, BLOCK - 1 : BLOCK]
    q_rows[32:64, :] = b_q
    w_rows[...] = jnp.exp2(b_end - b_q)
    e_rows[...] = jnp.broadcast_to(jnp.exp2(b_end), (32, 128))
    run_cols[...] = jnp.concatenate([run, b_run, jnp.zeros((64, BLOCK), F32)], axis=0).T
    for s in range(6):
        if s < 2:
            b_in, c_in = pbc[0, s], pbc[1, s]
        else:
            b, k = (s - 2) // 2, s % 2
            b_in = bbc[0, b, :, BLOCK * k : BLOCK * k + BLOCK]
            c_in = bbc[1, b, :, BLOCK * k : BLOCK * k + BLOCK]
        c_in = c_in.astype(F32)
        cols = jnp.concatenate([c_in, c_in, c_in, jnp.zeros((80, BLOCK), F32)], axis=0).T.astype(BF16)
        c_cols[s] = cols
        if s >= 2:
            b_cols[s - 2] = cols
        b_pad[s, 0:16, :] = b_in
        b_pad[s, 16:128, :] = jnp.zeros((112, BLOCK), BF16)
    start_parts[48:128, :] = jnp.zeros((80, 512), BF16)
    for ref in (state_parts, mid_parts):
        for i in range(ref.shape[0]):
            ref[i, 48:128, :] = jnp.zeros((80, 512), BF16)

    low256 = iota((BLOCK, 128), 1) < 64
    causal = iota((BLOCK, BLOCK), 1) <= iota((BLOCK, BLOCK), 0)

    def unit_pass(inner, lead, base, u, carry):
        s = jnp.where(u < 4, u // 2, u - 2)
        scores[...] = jnp.where(causal, dot(c_cols[s], b_pad[s]), 0.0)
        cols = pltpu.roll(run_cols[...], lax.rem(128 - 8 * u, 128), 1)
        q_unit = q_rows[pl.ds(pl.multiple_of(8 * u, 8), 8), :]
        for j in range(4):
            x_pair = xall[u, :, 128 * j : 128 * j + 128]
            products, spread = [], []
            for h in (2 * j, 2 * j + 1):
                col = jnp.broadcast_to(cols[:, h : h + 1], (BLOCK, 128))
                row = q_unit[h : h + 1, :]
                upper = jnp.exp2(jnp.minimum(col[:128] - row[:, :128], 0.0)) * scores[0:128, 0:128]
                left = jnp.exp2(jnp.minimum(col[128:] - row[:, :128], 0.0)) * scores[128:256, 0:128]
                right = jnp.exp2(jnp.minimum(col[128:] - row[:, 128:], 0.0)) * scores[128:256, 128:256]
                top = dot(upper.astype(BF16), x_pair[:128])
                low = dot(jnp.concatenate([left, right], axis=1).astype(BF16), x_pair)
                products.append(jnp.concatenate([top, low], axis=0))
                spread.append(col)
            inner[u - base, :, 128 * j : 128 * j + 128] = pair_of(products[0], products[1], low256)
            lead[u - base, :, 128 * j : 128 * j + 128] = jnp.exp2(pair_of(spread[0], spread[1], low256))
        return carry

    b_pass = functools.partial(unit_pass, b_inner, b_lead, 4)
    lax.fori_loop(0, 4, functools.partial(unit_pass, p_inner, p_lead, 0), 0)
    wait_for(xall.at[pl.ds(4, 4)], in_sem.at[2])
    lax.fori_loop(4, 8, b_pass, 0)

    wait_for(yfell.at[pl.ds(1, ny - 1)], dr)
    wait_for(yrecv.at[:, pl.ds(1, ny - 1)], yr)
    state = [jnp.zeros((16, 128), F32)] * 2
    fall = jnp.ones((2, 128), F32)
    for s in range(ny):
        slot = lax.rem(y - s + ny, ny)
        decay[s] = fall
        step = yfell[slot]
        for pr in range(2):
            back[s, 16 * pr : 16 * pr + 16, :] = state[pr]
            state[pr] = step[pr : pr + 1] * state[pr] + yrecv[pr, slot]
        fall = fall * step
    for pr in range(2):
        xsend[16 * pr : 16 * pr + 16, :] = state[pr]
    xfall[...] = fall

    def x_row_copy(k):
        there = lax.rem(x + k, nx)
        return pltpu.make_async_remote_copy(
            src_ref=xsend, dst_ref=xrecv.at[k], send_sem=xs, recv_sem=xr,
            device_id={"ctx_0": there}, device_id_type=MESH,
        )

    def x_fall_copy(k):
        there = lax.rem(x + k, nx)
        return pltpu.make_async_remote_copy(
            src_ref=xfall, dst_ref=xfell.at[k], send_sem=es, recv_sem=er,
            device_id={"ctx_0": there}, device_id_type=MESH,
        )

    def total_copy():
        return pltpu.make_async_remote_copy(
            src_ref=xsend, dst_ref=row_in.at[x, place], send_sem=fs.at[0], recv_sem=fr.at[0],
            device_id={"ctx_0": hub_x, "ctx_1": hub_y}, device_id_type=MESH,
        )

    def total_fall_copy():
        return pltpu.make_async_remote_copy(
            src_ref=xfall, dst_ref=row_fell.at[x, place], send_sem=fs.at[1], recv_sem=fr.at[1],
            device_id={"ctx_0": hub_x, "ctx_1": hub_y}, device_id_type=MESH,
        )

    @pl.when(from_hub)
    def _():
        total_copy().start()
        total_fall_copy().start()

    @pl.when(at_hub)
    def _():
        pltpu.make_async_copy(xsend, row_in.at[x, place], fr.at[0]).start()
        pltpu.make_async_copy(xfall, row_fell.at[x, place], fr.at[1]).start()

    for k in far_first(nx):
        x_row_copy(k).start()
        x_fall_copy(k).start()
    xrecv[0] = xsend[...]
    xfell[0] = xfall[...]

    if nx > 1:
        wait_for(xfell.at[pl.ds(1, nx - 1)], er)
        wait_for(xrecv.at[pl.ds(1, nx - 1)], xr)
    state = jnp.zeros((32, 128), F32)
    mine = state
    for s in range(nx):
        mine = jnp.where(x == s, state, mine)
        if s < nx - 1:
            slot = lax.rem(x - s + nx, nx)
            state = rows16(xfell[slot]) * state + xrecv[slot]

    def back_copy(k):
        there = lax.rem(y + k, ny)
        return pltpu.make_async_remote_copy(
            src_ref=back.at[there], dst_ref=before.at[k], send_sem=bs, recv_sem=br,
            device_id={"ctx_1": there}, device_id_type=MESH,
        )

    for s in range(ny):
        back[s] = back[s] + rows16(decay[s]) * mine
    for k in far_first(ny):
        back_copy(k).start()
    before[0] = back[y]

    def start_copy(to):
        return pltpu.make_async_remote_copy(
            src_ref=staged.at[to], dst_ref=start, send_sem=gs, recv_sem=gr,
            device_id={"pair": to}, device_id_type=MESH,
        )

    def chosen(flags, states):
        first = jnp.concatenate([flags, flags], axis=0) < 0.5
        return [jnp.where(first, state[0:16], state[16:32]) for state in states]

    @pl.when(is_hub)
    def _():
        wait_for(row_fell, fr.at[1])
        wait_for(row_in, fr.at[0])
        wait_for(prompts.at[pl.ds(0, nz - 1)], tr)
        states = []
        for i in range(4):
            state = jnp.zeros((32, 128), F32)
            for s in range(nx):
                state = rows16(row_fell[s, i]) * state + row_in[s, i]
            states.append(state)
        for to in range(nz):

            @pl.when(p != to)
            def _(to=to):
                for i, state in enumerate(chosen(prompts[to], states)):
                    staged[to, 16 * i : 16 * i + 16, :] = state
                start_copy(to).start()

        for i, state in enumerate(chosen(tile[...], states)):
            start[16 * i : 16 * i + 16, :] = state

    small[4].wait()
    for b in range(2):
        first, second = 2 * b, 2 * b + 1
        states = pair_states(
            bbc[0, b, :, 0:BLOCK].astype(F32),
            w_rows[16 * b : 16 * b + 8],
            xall,
            lambda group, b=b: (4 + 2 * b, 256 * group),
            8,
        )
        for j in range(4):
            store_parts(mid_parts.at[b], 128 * j, states[j])
        carried = dot(c_cols[3 + 2 * b], mid_parts[b])
        place_of = iota((BLOCK, 128), 0)
        for j in range(4):
            lanes = slice(128 * j, 128 * j + 128)
            fall = pair_of(e_rows[16 * b + 2 * j : 16 * b + 2 * j + 1], e_rows[16 * b + 2 * j + 1 : 16 * b + 2 * j + 2], low1)
            live = place_of < blen[b]
            b_inner[first, :, lanes] = jnp.where(live, b_inner[first, :, lanes], 0.0)
            b_lead[first, :, lanes] = jnp.where(live, b_lead[first, :, lanes], 0.0)
            live = place_of + BLOCK < blen[b]
            own = b_lead[second, :, lanes]
            b_inner[second, :, lanes] = jnp.where(live, b_inner[second, :, lanes] + own * carried[:, lanes], 0.0)
            b_lead[second, :, lanes] = jnp.where(live, own * fall, 0.0)

    wait_for(before.at[pl.ds(1, ny - 1)], br)
    for j in range(8):
        slot = lax.rem(y - holder(j) + ny, ny)
        for pr in range(2):
            store_parts(
                state_parts.at[2 * pr + j // 4], 128 * (j % 4), before[slot, 16 * pr : 16 * pr + 16, :]
            )
    for u in range(4):
        carried = dot(c_cols[u // 2], state_parts[u])
        prompt_outs[u] = (p_inner[u] + p_lead[u] * carried).astype(BF16)

    wait_for(ysend.at[:, pl.ds(0, ny - 1)], ys)
    wait_for(yfall.at[pl.ds(0, ny - 1)], ds)
    wait_for(back.at[pl.ds(0, ny - 1)], bs)
    if nx > 1:
        wait_for(xrecv.at[pl.ds(0, nx - 1)], xs)
        wait_for(xfell.at[pl.ds(0, nx - 1)], es)

    @pl.when(from_hub)
    def _():
        total_copy().wait_send()
        total_fall_copy().wait_send()

    @pl.when(not_hub)
    def _():
        tile_copy(p).wait_send()
        start_copy(0).wait_recv()

    for i in range(4):
        store_parts(start_parts, 128 * i, start[16 * i : 16 * i + 16, :])

    @pl.when(is_hub)
    def _():
        wait_for(staged.at[pl.ds(0, nz - 1)], gs)


def write_kernel(prompt_outs, b_inner, b_lead, start_parts, b_cols, py, by, outs, sem):
    copies = [
        pltpu.make_async_copy(prompt_outs.at[u], py.at[u // 2, :, pl.ds(512 * (u % 2), 512)], sem.at[u])
        for u in range(4)
    ]
    for copy in copies:
        copy.start()
    for u in range(4):
        outs[u] = (b_inner[u] + b_lead[u] * dot(b_cols[u], start_parts[...])).astype(BF16)
        copy = pltpu.make_async_copy(
            outs.at[u], by.at[u // 2, pl.ds(BLOCK * (u % 2), BLOCK), :], sem.at[4 + u]
        )
        copy.start()
        copies.append(copy)
    for copy in copies:
        copy.wait()


def body(nx, ny, nz, px, pbc, pld, bx, bbc, bld, bprompt, blen):
    any_space = pl.BlockSpec(memory_space=pl.ANY)
    vmem = pl.BlockSpec(memory_space=pltpu.VMEM)
    dma = pltpu.SemaphoreType.DMA
    between = [
        pltpu.VMEM((4, BLOCK, 512), BF16),
        pltpu.VMEM((4, BLOCK, 512), F32),
        pltpu.VMEM((4, BLOCK, 512), F32),
        pltpu.VMEM((128, 512), BF16),
        pltpu.VMEM((4, BLOCK, 128), BF16),
    ]
    kept = pl.pallas_call(
        functools.partial(kernel, nx, ny, nz),
        out_shape=between,
        in_specs=[pl.BlockSpec(memory_space=pltpu.HBM)] * 7 + [pl.BlockSpec(memory_space=pltpu.SMEM)],
        out_specs=[vmem] * 5,
        scratch_shapes=[
            pltpu.VMEM(pbc.shape, BF16),
            pltpu.VMEM(pld.shape, F32),
            pltpu.VMEM(bbc.shape, BF16),
            pltpu.VMEM(bld.shape, F32),
            pltpu.SMEM(blen.shape, jnp.int32),
            pltpu.VMEM((8, BLOCK, 512), BF16),
            pltpu.VMEM((4, BLOCK, 512), F32),
            pltpu.VMEM((4, BLOCK, 512), F32),
            pltpu.VMEM((BLOCK, BLOCK), F32),
            pltpu.VMEM((6, BLOCK, 128), BF16),
            pltpu.VMEM((6, 128, BLOCK), BF16),
            pltpu.VMEM((BLOCK, 128), F32),
            pltpu.VMEM((64, BLOCK), F32),
            pltpu.VMEM((32, BLOCK), F32),
            pltpu.VMEM((32, 128), F32),
            pltpu.VMEM((4, 128, 512), BF16),
            pltpu.VMEM((2, 128, 512), BF16),
            pltpu.VMEM((2, ny, 16, 128), F32),
            pltpu.VMEM((ny, 2, 128), F32),
            pltpu.VMEM((2, ny, 16, 128), F32),
            pltpu.VMEM((ny, 2, 128), F32),
            pltpu.VMEM((ny, 32, 128), F32),
            pltpu.VMEM((ny, 2, 128), F32),
            pltpu.VMEM((32, 128), F32),
            pltpu.VMEM((2, 128), F32),
            pltpu.VMEM((nx, 32, 128), F32),
            pltpu.VMEM((nx, 2, 128), F32),
            pltpu.VMEM((ny, 32, 128), F32),
            pltpu.VMEM((nx, 4, 32, 128), F32),
            pltpu.VMEM((nx, 4, 2, 128), F32),
            pltpu.VMEM((8, 128), F32),
            pltpu.VMEM((nz, 8, 128), F32),
            pltpu.VMEM((nz, 64, 128), F32),
            pltpu.VMEM((64, 128), F32),
            dma((8,)),
            dma, dma,
            dma, dma,
            dma, dma,
            dma, dma,
            dma, dma,
            dma((2,)), dma((2,)),
            dma, dma,
            dma, dma,
        ],
        compiler_params=pltpu.CompilerParams(
            collective_id=0, has_side_effects=True, vmem_limit_bytes=40 * 1024 * 1024
        ),
        name="layer",
    )(*[pltpu.with_memory_space_constraint(a, pltpu.HBM) for a in (px, pbc, pld, bx, bbc, bld, blen)], bprompt)
    return pl.pallas_call(
        write_kernel,
        out_shape=(jax.ShapeDtypeStruct(px.shape, BF16), jax.ShapeDtypeStruct(bx.shape, BF16)),
        in_specs=[vmem] * 5,
        out_specs=(any_space, any_space),
        scratch_shapes=[pltpu.VMEM((4, BLOCK, 512), BF16), dma((8,))],
        compiler_params=pltpu.CompilerParams(vmem_limit_bytes=16 * 1024 * 1024),
        name="write",
    )(*kept)


def solution(mesh):
    nx = 4
    ny, nz = mesh.shape["ctx"] // nx, mesh.shape["pair"]
    finer = Mesh(mesh.devices.reshape(nx, ny, nz), ("ctx_0", "ctx_1", "pair"))
    return jax.shard_map(
        functools.partial(body, nx, ny, nz),
        mesh=finer,
        in_specs=(
            P(None, CTX, "pair"),
            P(None, None, None, CTX),
            P(None, "pair", CTX),
            P("pair", None, CTX),
            P(None, "pair", None, None),
            P("pair", CTX, None),
            P("pair"),
            P("pair"),
        ),
        out_specs=(P(None, CTX, "pair"), P("pair", None, CTX)),
        check_vma=False,
    )
```

```python
import functools

import jax
import jax.numpy as jnp
from jax import lax
from jax.experimental import pallas as pl
from jax.experimental.pallas import tpu as pltpu
from jax.sharding import Mesh
from jax.sharding import PartitionSpec as P

MESH = pl.DeviceIdType.MESH
CTX = ("ctx_0", "ctx_1")
F32 = jnp.float32
BF16 = jnp.bfloat16
BLOCK = 256
LOG2E = 1.4426950408889634


def iota(shape, dim):
    return lax.broadcasted_iota(jnp.int32, shape, dim)


def dot(a, b):
    return jnp.dot(a, b, preferred_element_type=F32)


def far_first(n):
    return sorted(range(1, n), key=lambda k: -min(k, n - k))


def three_parts(a):
    hi = a.astype(BF16)
    rest = a - hi.astype(F32)
    mid = rest.astype(BF16)
    low = (rest - mid.astype(F32)).astype(BF16)
    return hi, mid, low


def running_sums(rows):
    until = (iota((BLOCK, BLOCK), 0) <= iota((BLOCK, BLOCK), 1)).astype(F32).astype(BF16)
    count = rows.shape[0]
    sums = dot(jnp.concatenate(three_parts(rows), axis=0), until)
    total = sums[:count] + (sums[count : 2 * count] + sums[2 * count :])
    return total * LOG2E


def log_gain(rows):
    z = 2.0 * rows
    series = 1.0 / 362880.0
    for factor in (40320.0, 5040.0, 720.0, 120.0, 24.0, 6.0, 2.0, 1.0):
        series = series * z + 1.0 / factor
    squared = jnp.where(z > -0.5, -z * series, 1.0 - jnp.exp(z))
    return jnp.where(squared > 0.0, (0.5 * LOG2E) * jnp.log(squared), -1e30)


def pair_of(even, odd, low_lanes):
    return jnp.where(low_lanes, even, odd)


def rows16(tile):
    return jnp.concatenate(
        [jnp.broadcast_to(tile[0:1], (16, 128)), jnp.broadcast_to(tile[1:2], (16, 128))], axis=0
    )


def pair_states(b_rows, weights, x_ref, unit_of, heads):
    low16 = iota((16, 128), 1) < 64
    found = []
    for group in range(heads // 4):
        push = jnp.concatenate(
            [b_rows * weights[4 * group + i : 4 * group + i + 1, :] for i in range(4)], axis=0
        ).astype(BF16)
        unit, lane = unit_of(group)
        sums = dot(push, x_ref[unit, :, lane : lane + 256])
        for i in range(2):
            part = sums[32 * i : 32 * i + 32, 128 * i : 128 * i + 128]
            found.append(pair_of(part[0:16], part[16:32], low16))
    return found


def wait_for(ref, sem):
    pltpu.make_async_copy(ref, ref, sem).wait()


def store_parts(ref, lane, state):
    for place, part in enumerate(three_parts(state)):
        ref[16 * place : 16 * place + 16, lane : lane + 128] = part


def kernel(
    nx, ny, nz,
    px, pbc_in, pld_in, bx, bbc_in, bld_in, blen_in, bprompt,
    prompt_outs, b_inner, b_lead, start_parts, b_cols,
    pbc, pld, bbc, bld, blen,
    xall, p_inner, p_lead, scores, c_cols, b_pad, run_cols, q_rows, w_rows, e_rows,
    state_parts, mid_parts,
    ysend, yfall, yrecv, yfell, back, decay, xsend, xfall, xrecv, xfell, before, row_in, row_fell,
    tile, prompts, staged, start,
    in_sem, ys, yr, ds, dr, xs, xr, es, er, bs, br, fs, fr, ts, tr, gs, gr,
):
    x, y, p = lax.axis_index("ctx_0"), lax.axis_index("ctx_1"), lax.axis_index("pair")
    hub = (x * ny + y) // 2
    is_hub = p == hub
    not_hub = p != hub

    barrier = pltpu.get_barrier_semaphore()

    def greet(where):
        pl.semaphore_signal(barrier, inc=1, device_id=where, device_id_type=MESH)

    first_hub = lax.rem(2 * p, ny)

    def holder(j):
        return lax.rem(first_hub + ny + (j - 3 if j >= 4 else -j), ny)

    def held_by(at):
        far = lax.rem(at - first_hub + ny, ny)
        return jnp.where(jnp.logical_and(far >= 1, far <= 4), far + 3, lax.rem(ny - far, ny))

    mine_j = held_by(y)
    place = lax.rem(mine_j, 4)
    hub_x = (2 * p) // ny
    hub_y = lax.rem(first_hub + mine_j // 4, ny)
    other_row = x != hub_x
    at_hub = jnp.logical_and(x == hub_x, y == hub_y)
    from_hub = jnp.logical_not(at_hub)
    for k in range(1, ny):
        greet({"ctx_1": lax.rem(y + k, ny)})
    for k in range(1, nx):
        greet({"ctx_0": lax.rem(x + k, nx)})

    @pl.when(is_hub)
    def _():
        for k in range(1, nz):
            greet({"pair": lax.rem(p + k, nz)})
        side = 2 * (y - first_hub) - 1
        for k in range(1, nx):
            for i in range(4):
                greet({"ctx_0": lax.rem(x + k, nx), "ctx_1": lax.rem(y + side * i + ny, ny)})

    @pl.when(other_row)
    def _():
        greet({"ctx_0": hub_x, "ctx_1": hub_y})

    @pl.when(not_hub)
    def _():
        greet({"pair": hub})

    small = [
        pltpu.make_async_copy(source, target, in_sem.at[3 + i])
        for i, (source, target) in enumerate(
            [(pld_in, pld), (pbc_in, pbc), (bld_in, bld), (bbc_in, bbc), (blen_in, blen)]
        )
    ]

    def x_copy(u):
        if u < 4:
            source = px.at[u // 2, :, pl.ds(512 * (u % 2), 512)]
        else:
            source = bx.at[(u - 4) // 2, pl.ds(BLOCK * (u % 2), BLOCK), :]
        return pltpu.make_async_copy(source, xall.at[u], in_sem.at[min(u // 2, 2)])

    small[0].start()
    small[1].start()
    for u in range(4):
        x_copy(u).start()
    for copy in small[2:]:
        copy.start()
    for u in range(4, 8):
        x_copy(u).start()

    def y_copy(pr, k):
        there = lax.rem(y + k, ny)
        return pltpu.make_async_remote_copy(
            src_ref=ysend.at[pr, held_by(there)], dst_ref=yrecv.at[pr, k],
            send_sem=ys, recv_sem=yr,
            device_id={"ctx_1": there}, device_id_type=MESH,
        )

    def fall_copy(k):
        there = lax.rem(y + k, ny)
        return pltpu.make_async_remote_copy(
            src_ref=yfall.at[held_by(there)], dst_ref=yfell.at[k], send_sem=ds, recv_sem=dr,
            device_id={"ctx_1": there}, device_id_type=MESH,
        )

    def tile_copy(of):
        return pltpu.make_async_remote_copy(
            src_ref=tile, dst_ref=prompts.at[of], send_sem=ts, recv_sem=tr,
            device_id={"pair": hub}, device_id_type=MESH,
        )

    low8 = iota((8, 128), 1) < 64

    small[0].wait()
    rows = jnp.concatenate([pld[0], pld[1]], axis=0)
    run = running_sums(rows)
    q = run - log_gain(rows)
    run_end = run[:, BLOCK - 1 : BLOCK]
    weights = jnp.exp2(run_end - q)
    ends = jnp.broadcast_to(jnp.exp2(run_end), (32, 128))
    q_rows[0:32, :] = q
    low1 = iota((1, 128), 1) < 64
    for pr in range(2):
        for j in range(8):
            h = 16 * pr + 2 * j
            yfall[j, pr : pr + 1, :] = pair_of(ends[h : h + 1], ends[h + 1 : h + 2], low1)
    small[1].wait()
    for pr in range(2):
        wait_for(xall.at[pl.ds(2 * pr, 2)], in_sem.at[pr])
        states = pair_states(
            pbc[0, pr].astype(F32),
            weights[16 * pr : 16 * pr + 16],
            xall,
            lambda group, pr=pr: (2 * pr + group // 2, 256 * (group % 2)),
            16,
        )
        for j in range(8):
            ysend[pr, j] = states[j]
        if pr == 0:
            more = (nz - 2 + 4 * (nx - 1)) * is_hub.astype(jnp.int32) + other_row.astype(jnp.int32)
            pl.semaphore_wait(barrier, ny - 1 + nx - 1 + 1 + more)
        for k in far_first(ny):
            y_copy(pr, k).start()
    for k in far_first(ny):
        fall_copy(k).start()
    tile[...] = jnp.full((8, 128), bprompt[0], jnp.int32).astype(F32)

    @pl.when(not_hub)
    def _():
        tile_copy(p).start()

    for pr in range(2):
        yrecv[pr, 0] = ysend[pr, mine_j]
    yfell[0] = yfall[mine_j]

    small[2].wait()
    small[3].wait()
    b_rows_in = [bld[b, :, BLOCK * k : BLOCK * k + BLOCK] for b in range(2) for k in range(2)]
    rows = jnp.concatenate(b_rows_in, axis=0)
    b_run = running_sums(rows)
    b_q = b_run - log_gain(rows)
    b_end = b_run[:, BLOCK - 1 : BLOCK]
    q_rows[32:64, :] = b_q
    w_rows[...] = jnp.exp2(b_end - b_q)
    e_rows[...] = jnp.broadcast_to(jnp.exp2(b_end), (32, 128))
    run_cols[...] = jnp.concatenate([run, b_run, jnp.zeros((64, BLOCK), F32)], axis=0).T
    for s in range(6):
        if s < 2:
            b_in, c_in = pbc[0, s], pbc[1, s]
        else:
            b, k = (s - 2) // 2, s % 2
            b_in = bbc[0, b, :, BLOCK * k : BLOCK * k + BLOCK]
            c_in = bbc[1, b, :, BLOCK * k : BLOCK * k + BLOCK]
        c_in = c_in.astype(F32)
        cols = jnp.concatenate([c_in, c_in, c_in, jnp.zeros((80, BLOCK), F32)], axis=0).T.astype(BF16)
        c_cols[s] = cols
        if s >= 2:
            b_cols[s - 2] = cols
        b_pad[s, 0:16, :] = b_in
        b_pad[s, 16:128, :] = jnp.zeros((112, BLOCK), BF16)
    start_parts[48:128, :] = jnp.zeros((80, 512), BF16)
    for ref in (state_parts, mid_parts):
        for i in range(ref.shape[0]):
            ref[i, 48:128, :] = jnp.zeros((80, 512), BF16)

    low256 = iota((BLOCK, 128), 1) < 64
    causal = iota((BLOCK, BLOCK), 1) <= iota((BLOCK, BLOCK), 0)

    def unit_pass(inner, lead, base, u, carry):
        s = jnp.where(u < 4, u // 2, u - 2)
        scores[...] = jnp.where(causal, dot(c_cols[s], b_pad[s]), 0.0)
        cols = pltpu.roll(run_cols[...], lax.rem(128 - 8 * u, 128), 1)
        q_unit = q_rows[pl.ds(pl.multiple_of(8 * u, 8), 8), :]
        for j in range(4):
            x_pair = xall[u, :, 128 * j : 128 * j + 128]
            products, spread = [], []
            for h in (2 * j, 2 * j + 1):
                col = jnp.broadcast_to(cols[:, h : h + 1], (BLOCK, 128))
                row = q_unit[h : h + 1, :]
                upper = jnp.exp2(jnp.minimum(col[:128] - row[:, :128], 0.0)) * scores[0:128, 0:128]
                left = jnp.exp2(jnp.minimum(col[128:] - row[:, :128], 0.0)) * scores[128:256, 0:128]
                right = jnp.exp2(jnp.minimum(col[128:] - row[:, 128:], 0.0)) * scores[128:256, 128:256]
                top = dot(upper.astype(BF16), x_pair[:128])
                low = dot(jnp.concatenate([left, right], axis=1).astype(BF16), x_pair)
                products.append(jnp.concatenate([top, low], axis=0))
                spread.append(col)
            inner[u - base, :, 128 * j : 128 * j + 128] = pair_of(products[0], products[1], low256)
            lead[u - base, :, 128 * j : 128 * j + 128] = jnp.exp2(pair_of(spread[0], spread[1], low256))
        return carry

    b_pass = functools.partial(unit_pass, b_inner, b_lead, 4)
    lax.fori_loop(0, 4, functools.partial(unit_pass, p_inner, p_lead, 0), 0)
    wait_for(xall.at[pl.ds(4, 4)], in_sem.at[2])
    lax.fori_loop(4, 8, b_pass, 0)

    wait_for(yfell.at[pl.ds(1, ny - 1)], dr)
    wait_for(yrecv.at[:, pl.ds(1, ny - 1)], yr)
    state = [jnp.zeros((16, 128), F32)] * 2
    fall = jnp.ones((2, 128), F32)
    for s in range(ny):
        slot = lax.rem(y - s + ny, ny)
        decay[s] = fall
        step = yfell[slot]
        for pr in range(2):
            back[s, 16 * pr : 16 * pr + 16, :] = state[pr]
            state[pr] = step[pr : pr + 1] * state[pr] + yrecv[pr, slot]
        fall = fall * step
    for pr in range(2):
        xsend[16 * pr : 16 * pr + 16, :] = state[pr]
    xfall[...] = fall

    def x_row_copy(k):
        there = lax.rem(x + k, nx)
        return pltpu.make_async_remote_copy(
            src_ref=xsend, dst_ref=xrecv.at[k], send_sem=xs, recv_sem=xr,
            device_id={"ctx_0": there}, device_id_type=MESH,
        )

    def x_fall_copy(k):
        there = lax.rem(x + k, nx)
        return pltpu.make_async_remote_copy(
            src_ref=xfall, dst_ref=xfell.at[k], send_sem=es, recv_sem=er,
            device_id={"ctx_0": there}, device_id_type=MESH,
        )

    def total_copy():
        return pltpu.make_async_remote_copy(
            src_ref=xsend, dst_ref=row_in.at[x, place], send_sem=fs.at[0], recv_sem=fr.at[0],
            device_id={"ctx_0": hub_x, "ctx_1": hub_y}, device_id_type=MESH,
        )

    def total_fall_copy():
        return pltpu.make_async_remote_copy(
            src_ref=xfall, dst_ref=row_fell.at[x, place], send_sem=fs.at[1], recv_sem=fr.at[1],
            device_id={"ctx_0": hub_x, "ctx_1": hub_y}, device_id_type=MESH,
        )

    @pl.when(from_hub)
    def _():
        total_copy().start()
        total_fall_copy().start()

    @pl.when(at_hub)
    def _():
        pltpu.make_async_copy(xsend, row_in.at[x, place], fr.at[0]).start()
        pltpu.make_async_copy(xfall, row_fell.at[x, place], fr.at[1]).start()

    for k in far_first(nx):
        x_row_copy(k).start()
        x_fall_copy(k).start()
    xrecv[0] = xsend[...]
    xfell[0] = xfall[...]

    if nx > 1:
        wait_for(xfell.at[pl.ds(1, nx - 1)], er)
        wait_for(xrecv.at[pl.ds(1, nx - 1)], xr)
    state = jnp.zeros((32, 128), F32)
    mine = state
    for s in range(nx):
        mine = jnp.where(x == s, state, mine)
        if s < nx - 1:
            slot = lax.rem(x - s + nx, nx)
            state = rows16(xfell[slot]) * state + xrecv[slot]

    def back_copy(k):
        there = lax.rem(y + k, ny)
        return pltpu.make_async_remote_copy(
            src_ref=back.at[there], dst_ref=before.at[k], send_sem=bs, recv_sem=br,
            device_id={"ctx_1": there}, device_id_type=MESH,
        )

    for s in range(ny):
        back[s] = back[s] + rows16(decay[s]) * mine
    for k in far_first(ny):
        back_copy(k).start()
    before[0] = back[y]

    def start_copy(to):
        return pltpu.make_async_remote_copy(
            src_ref=staged.at[to], dst_ref=start, send_sem=gs, recv_sem=gr,
            device_id={"pair": to}, device_id_type=MESH,
        )

    def chosen(flags, states):
        first = jnp.concatenate([flags, flags], axis=0) < 0.5
        return [jnp.where(first, state[0:16], state[16:32]) for state in states]

    @pl.when(is_hub)
    def _():
        wait_for(row_fell, fr.at[1])
        wait_for(row_in, fr.at[0])
        wait_for(prompts.at[pl.ds(0, nz - 1)], tr)
        states = []
        for i in range(4):
            state = jnp.zeros((32, 128), F32)
            for s in range(nx):
                state = rows16(row_fell[s, i]) * state + row_in[s, i]
            states.append(state)
        for to in range(nz):

            @pl.when(p != to)
            def _(to=to):
                for i, state in enumerate(chosen(prompts[to], states)):
                    staged[to, 16 * i : 16 * i + 16, :] = state
                start_copy(to).start()

        for i, state in enumerate(chosen(tile[...], states)):
            start[16 * i : 16 * i + 16, :] = state

    small[4].wait()
    for b in range(2):
        first, second = 2 * b, 2 * b + 1
        states = pair_states(
            bbc[0, b, :, 0:BLOCK].astype(F32),
            w_rows[16 * b : 16 * b + 8],
            xall,
            lambda group, b=b: (4 + 2 * b, 256 * group),
            8,
        )
        for j in range(4):
            store_parts(mid_parts.at[b], 128 * j, states[j])
        carried = dot(c_cols[3 + 2 * b], mid_parts[b])
        place_of = iota((BLOCK, 128), 0)
        for j in range(4):
            lanes = slice(128 * j, 128 * j + 128)
            fall = pair_of(e_rows[16 * b + 2 * j : 16 * b + 2 * j + 1], e_rows[16 * b + 2 * j + 1 : 16 * b + 2 * j + 2], low1)
            live = place_of < blen[b]
            b_inner[first, :, lanes] = jnp.where(live, b_inner[first, :, lanes], 0.0)
            b_lead[first, :, lanes] = jnp.where(live, b_lead[first, :, lanes], 0.0)
            live = place_of + BLOCK < blen[b]
            own = b_lead[second, :, lanes]
            b_inner[second, :, lanes] = jnp.where(live, b_inner[second, :, lanes] + own * carried[:, lanes], 0.0)
            b_lead[second, :, lanes] = jnp.where(live, own * fall, 0.0)

    wait_for(before.at[pl.ds(1, ny - 1)], br)
    for j in range(8):
        slot = lax.rem(y - holder(j) + ny, ny)
        for pr in range(2):
            store_parts(
                state_parts.at[2 * pr + j // 4], 128 * (j % 4), before[slot, 16 * pr : 16 * pr + 16, :]
            )
    for u in range(4):
        carried = dot(c_cols[u // 2], state_parts[u])
        prompt_outs[u] = (p_inner[u] + p_lead[u] * carried).astype(BF16)

    wait_for(ysend.at[:, pl.ds(0, ny - 1)], ys)
    wait_for(yfall.at[pl.ds(0, ny - 1)], ds)
    wait_for(back.at[pl.ds(0, ny - 1)], bs)
    if nx > 1:
        wait_for(xrecv.at[pl.ds(0, nx - 1)], xs)
        wait_for(xfell.at[pl.ds(0, nx - 1)], es)

    @pl.when(from_hub)
    def _():
        total_copy().wait_send()
        total_fall_copy().wait_send()

    @pl.when(not_hub)
    def _():
        tile_copy(p).wait_send()
        start_copy(0).wait_recv()

    for i in range(4):
        store_parts(start_parts, 128 * i, start[16 * i : 16 * i + 16, :])

    @pl.when(is_hub)
    def _():
        wait_for(staged.at[pl.ds(0, nz - 1)], gs)


def write_kernel(prompt_outs, b_inner, b_lead, start_parts, b_cols, py, by, outs, sem):
    for u in range(4):
        pltpu.make_async_copy(
            prompt_outs.at[u], py.at[u // 2, :, pl.ds(512 * (u % 2), 512)], sem.at[0]
        ).start()
    for u in range(4):
        for row in range(0, BLOCK, 128):
            rows = slice(row, row + 128)
            for lane in range(0, 512, 256):
                lanes = slice(lane, lane + 256)
                carried = dot(b_cols[u, rows, :], start_parts[:, lanes])
                outs[u, rows, lanes] = (b_inner[u, rows, lanes] + b_lead[u, rows, lanes] * carried).astype(BF16)
            pltpu.make_async_copy(
                outs.at[u, pl.ds(row, 128), :],
                by.at[u // 2, pl.ds(BLOCK * (u % 2) + row, 128), :],
                sem.at[1],
            ).start()
    wait_for(prompt_outs, sem.at[0])
    wait_for(outs, sem.at[1])


def body(nx, ny, nz, px, pbc, pld, bx, bbc, bld, bprompt, blen):
    any_space = pl.BlockSpec(memory_space=pl.ANY)
    vmem = pl.BlockSpec(memory_space=pltpu.VMEM)
    dma = pltpu.SemaphoreType.DMA
    between = [
        pltpu.VMEM((4, BLOCK, 512), BF16),
        pltpu.VMEM((4, BLOCK, 512), F32),
        pltpu.VMEM((4, BLOCK, 512), F32),
        pltpu.VMEM((128, 512), BF16),
        pltpu.VMEM((4, BLOCK, 128), BF16),
    ]
    kept = pl.pallas_call(
        functools.partial(kernel, nx, ny, nz),
        out_shape=between,
        in_specs=[pl.BlockSpec(memory_space=pltpu.HBM)] * 7 + [pl.BlockSpec(memory_space=pltpu.SMEM)],
        out_specs=[vmem] * 5,
        scratch_shapes=[
            pltpu.VMEM(pbc.shape, BF16),
            pltpu.VMEM(pld.shape, F32),
            pltpu.VMEM(bbc.shape, BF16),
            pltpu.VMEM(bld.shape, F32),
            pltpu.SMEM(blen.shape, jnp.int32),
            pltpu.VMEM((8, BLOCK, 512), BF16),
            pltpu.VMEM((4, BLOCK, 512), F32),
            pltpu.VMEM((4, BLOCK, 512), F32),
            pltpu.VMEM((BLOCK, BLOCK), F32),
            pltpu.VMEM((6, BLOCK, 128), BF16),
            pltpu.VMEM((6, 128, BLOCK), BF16),
            pltpu.VMEM((BLOCK, 128), F32),
            pltpu.VMEM((64, BLOCK), F32),
            pltpu.VMEM((32, BLOCK), F32),
            pltpu.VMEM((32, 128), F32),
            pltpu.VMEM((4, 128, 512), BF16),
            pltpu.VMEM((2, 128, 512), BF16),
            pltpu.VMEM((2, ny, 16, 128), F32),
            pltpu.VMEM((ny, 2, 128), F32),
            pltpu.VMEM((2, ny, 16, 128), F32),
            pltpu.VMEM((ny, 2, 128), F32),
            pltpu.VMEM((ny, 32, 128), F32),
            pltpu.VMEM((ny, 2, 128), F32),
            pltpu.VMEM((32, 128), F32),
            pltpu.VMEM((2, 128), F32),
            pltpu.VMEM((nx, 32, 128), F32),
            pltpu.VMEM((nx, 2, 128), F32),
            pltpu.VMEM((ny, 32, 128), F32),
            pltpu.VMEM((nx, 4, 32, 128), F32),
            pltpu.VMEM((nx, 4, 2, 128), F32),
            pltpu.VMEM((8, 128), F32),
            pltpu.VMEM((nz, 8, 128), F32),
            pltpu.VMEM((nz, 64, 128), F32),
            pltpu.VMEM((64, 128), F32),
            dma((8,)),
            dma, dma,
            dma, dma,
            dma, dma,
            dma, dma,
            dma, dma,
            dma((2,)), dma((2,)),
            dma, dma,
            dma, dma,
        ],
        compiler_params=pltpu.CompilerParams(
            collective_id=0, has_side_effects=True, vmem_limit_bytes=40 * 1024 * 1024
        ),
        name="layer",
    )(*[pltpu.with_memory_space_constraint(a, pltpu.HBM) for a in (px, pbc, pld, bx, bbc, bld, blen)], bprompt)
    return pl.pallas_call(
        write_kernel,
        out_shape=(jax.ShapeDtypeStruct(px.shape, BF16), jax.ShapeDtypeStruct(bx.shape, BF16)),
        in_specs=[vmem] * 5,
        out_specs=(any_space, any_space),
        scratch_shapes=[pltpu.VMEM((4, BLOCK, 512), BF16), dma((2,))],
        compiler_params=pltpu.CompilerParams(vmem_limit_bytes=16 * 1024 * 1024),
        name="write",
    )(*kept)


def solution(mesh):
    nx = 4
    ny, nz = mesh.shape["ctx"] // nx, mesh.shape["pair"]
    finer = Mesh(mesh.devices.reshape(nx, ny, nz), ("ctx_0", "ctx_1", "pair"))
    return jax.shard_map(
        functools.partial(body, nx, ny, nz),
        mesh=finer,
        in_specs=(
            P(None, CTX, "pair"),
            P(None, None, None, CTX),
            P(None, "pair", CTX),
            P("pair", None, CTX),
            P(None, "pair", None, None),
            P("pair", CTX, None),
            P("pair"),
            P("pair"),
        ),
        out_specs=(P(None, CTX, "pair"), P("pair", None, CTX)),
        check_vma=False,
    )
```
